512 devices in a mesh: row: 32 (over z, y_lo), col: 4 (over y_hi, core), head: 4 (over x).
Axes of the slice: x: 4, y: 8 (y_hi: 2, y_lo: 4; y = y_hi * 4 + y_lo), z: 8, core: 2. Of those that a mesh axis runs over, the one named last changes fastest.
Arguments:
- tokens: bfloat16 [512, 128, 1024], P(('row', 'head'), 'col'), may hold values from -6 to 6
- valid: int32 [512, 128], P('row', 'col'), may hold values 0 or 1
- gain: float32 [1024], replicated, may hold values from 0.1 to 1.9
- w_qkv: bfloat16 [1024, 3, 1024], P(None, None, 'head'), may hold values from -0.1875 to 0.1875
- w_proj: bfloat16 [1024, 1024], P('head'), may hold values from -0.1875 to 0.1875
- rel_table: float32 [225, 16], P(None, 'head'), may hold values from -4 to 300
- cotangent: bfloat16 [512, 128, 1024], P(('row', 'head'), 'col'), may hold values from -24 to 24
Outputs:
- mixed: bfloat16 [512, 128, 1024], P(('row', 'head'), 'col')
- token_gradient: bfloat16 [512, 128, 1024], P(('row', 'head'), 'col')
- proj_grad: float32 [1024, 1024], P('head', ('row', 'col'))
- table_grad: float32 [225, 16], P(None, 'head')
The draws below stay inside these ranges and needn't reach their ends.
All inputs are finite; a program needn't handle non-finite values. No bound on the sum of `valid` on one device may be relied on, other than what follows from the above.
Results may differ from the reference program's by a relative error of at most 0.0078.
Values may be sent and summed in bfloat16 or wider, within the bound.
No kernel may reach another device: no remote copies, remote signals or barrier semaphores. Data moves between devices by JAX's collectives and lax.ppermute only.
A program may use at most 64 MiB of HBM per device.

```python
import math
import jax
import jax.numpy as jnp
from jax import lax

D = 1024
HEADS = 16
HD = 64
WIN = 8
SHIFT = 4
H = 512
W = 128
N_HEAD = 4


def draw_rel_table(key, part):
    first = jax.random.fold_in(key, 0)
    count = (2 * WIN - 1) * (2 * WIN - 1)
    return jnp.clip(jax.random.normal(first, (count, HEADS), jnp.float32), -4.0, 4.0)


def place_ends(result, stream_key, least, top_value):
    dims = result.shape
    spot = [jax.random.randint(jax.random.fold_in(stream_key, axis), (), 0, dims[axis]) for axis in range(len(dims))]
    result = result.at[tuple(spot)].set(least)
    longest = dims.index(max(dims))
    spot[longest] = (spot[longest] + 1) % dims[longest]
    return result.at[tuple(spot)].set(top_value)


def strengthened(drawn, rng, source, target, parts, factor):
    def block_of(dim):
        return (jnp.arange(drawn.shape[dim]) // (drawn.shape[dim] // parts)).reshape((-1,) + (1,) * (drawn.ndim - 1 - dim))

    one_side = jax.random.permutation(rng, parts)[block_of(target)]
    far = (block_of(target) + parts // 2) % parts
    return jnp.where((block_of(source) == one_side) | (block_of(source) == far), factor * drawn, drawn)


def steps_of(rng, extent, cuts, smallest, largest):
    level = 1.0
    for axis_at, parts in cuts:
        draws = jax.random.uniform(jax.random.fold_in(jax.random.fold_in(rng, 6), axis_at), (parts,), jnp.float32, smallest / len(cuts), largest / len(cuts))
        level = level * jnp.repeat(jnp.exp(draws), extent[axis_at] // parts).reshape((-1,) + (1,) * (len(extent) - 1 - axis_at))
    return level


def scatter_about(stream_key, extent, deviation, most, pieces=(), kind=jnp.bfloat16):
    array = jax.random.normal(stream_key, extent, jnp.float32) * deviation
    if len(pieces) > 0:
        array = steps_of(stream_key, extent, pieces, -0.22, 0.18) * array
    return jnp.clip(array, min=-most, max=most).astype(kind)


def noise_with(stream_key, dims, deviation, bound, pieces, heavy, held_as=jnp.bfloat16):
    values = deviation * jax.random.normal(stream_key, dims, jnp.float32)
    if pieces:
        values = values * steps_of(stream_key, dims, pieces, -0.22, 0.18)
    return jnp.clip(strengthened(values, jax.random.fold_in(stream_key, 3), *heavy), -bound, bound).astype(held_as)


def setup_inputs(seed: int = 0) -> dict:
    streams_of = jax.random.split(jax.random.key(seed), 8)
    return {
        "tokens": scatter_about(streams_of[0], (H, W, D), 1.0, 6.0, ((0, 128), (1, 4))),
        "valid": place_ends((jax.random.randint(streams_of[1], (H, W), 0, 4) < 3).astype(jnp.int32), jax.random.fold_in(streams_of[1], 1), 0, 1),
        "gain": jnp.clip(1.0 + 0.18 * jax.random.normal(streams_of[2], (D,), jnp.float32), 0.1, 1.9),
        "w_qkv": scatter_about(streams_of[3], (D, 3, D), D ** -0.5, 0.1875, ((2, 4),)),
        "w_proj": scatter_about(streams_of[4], (D, D), D ** -0.5, 0.1875, ((0, 4),)),
        "rel_table": draw_rel_table(jax.random.fold_in(streams_of[7], 71), 0),
        "cotangent": noise_with(streams_of[6], (H, W, D), 1.0, 24.0, ((0, 128), (1, 4)), (0, 2, 128, 5.5)),
    }


EPS = 1e-05
HIGH = lax.Precision.HIGHEST

def region(index, grand_total):
    return jnp.where(index < grand_total - WIN, 0, jnp.where(index < grand_total - SHIFT, 1, 2)).astype(jnp.int32)

def offsets():
    span = 2 * WIN - 1
    pos = jnp.arange(WIN * WIN, dtype=jnp.int32)
    prow = pos // WIN
    pcol = pos % WIN
    index = (prow[:, None] - prow[None, :] + WIN - 1) * span + (pcol[:, None] - pcol[None, :] + WIN - 1)
    table_ids = jnp.arange(span * span, dtype=jnp.int32)
    return (index[:, :, None] == table_ids[None, None, :]).astype(jnp.float32).reshape(WIN * WIN * WIN * WIN, span * span)

def to_windows(block):
    nrow, ncol, heads, depth = block.shape
    block = block.reshape(nrow // WIN, WIN, ncol // WIN, WIN, heads, depth).transpose(0, 2, 4, 1, 3, 5)
    return block.reshape(nrow // WIN * (ncol // WIN), heads, WIN * WIN, depth)

def from_windows(block, nrow, ncol):
    count, heads, posn, depth = block.shape
    block = block.reshape(nrow // WIN, ncol // WIN, heads, WIN, WIN, depth).transpose(0, 3, 1, 4, 2, 5)
    return block.reshape(nrow, ncol, heads * depth)

def attend(qkv, grad, labels, valid, bias, onehot):
    nrow, ncol = labels.shape
    feature_width = qkv.shape[3]
    heads = feature_width // HD
    scale = HD ** (-0.5)
    query = to_windows(qkv[:, :, 0].reshape(nrow, ncol, heads, HD)).astype(jnp.float32)
    key = to_windows(qkv[:, :, 1].reshape(nrow, ncol, heads, HD)).astype(jnp.float32)
    value = to_windows(qkv[:, :, 2].reshape(nrow, ncol, heads, HD)).astype(jnp.float32)
    dout = to_windows(grad.reshape(nrow, ncol, heads, HD)).astype(jnp.float32)
    lab_win = to_windows(labels[:, :, None, None])[:, 0, :, 0]
    val_win = to_windows(valid[:, :, None, None])[:, 0, :, 0]
    diagonal = jnp.eye(WIN * WIN, dtype=bool)
    allowed = (lab_win[:, :, None] == lab_win[:, None, :]) & ((val_win[:, None, :] == 1) | diagonal[None])
    scores = jnp.einsum('wiqd,wikd->wiqk', query, key) * scale + bias[None]
    scores = jnp.where(allowed[:, None], scores, -1e+30)
    top = lax.optimization_barrier(jnp.max(scores, -1, keepdims=True))
    expo = jnp.exp(scores - top)
    prob = expo / lax.optimization_barrier(jnp.sum(expo, -1, keepdims=True))
    prob_b = prob.astype(jnp.bfloat16).astype(jnp.float32)
    attended = jnp.einsum('wiqk,wikd->wiqd', prob_b, value).astype(jnp.bfloat16)
    dprob = jnp.einsum('wiqd,wikd->wiqk', dout, value)
    dvalue = jnp.einsum('wiqk,wiqd->wikd', prob_b, dout).astype(jnp.bfloat16)
    dscore = prob * (dprob - lax.optimization_barrier(jnp.sum(prob * dprob, -1, keepdims=True)))
    dscore_b = dscore.astype(jnp.bfloat16).astype(jnp.float32)
    dquery = (jnp.einsum('wiqk,wikd->wiqd', dscore_b, key) * scale).astype(jnp.bfloat16)
    dkey = (jnp.einsum('wiqk,wiqd->wikd', dscore_b, query) * scale).astype(jnp.bfloat16)
    summed = lax.optimization_barrier(jnp.sum(dscore, 0)).transpose(1, 2, 0).reshape(WIN * WIN * WIN * WIN, heads)
    tgrad = jnp.dot(onehot.T, summed, precision=HIGH)
    grads = jnp.stack([from_windows(dquery, nrow, ncol), from_windows(dkey, nrow, ncol), from_windows(dvalue, nrow, ncol)], 2)
    return (from_windows(attended, nrow, ncol), grads, tgrad)

def reference(tokens, valid, gain, w_qkv, w_proj, rel_table, cotangent):
    nrow, ncol, feature_width = tokens.shape
    grand_total = nrow * ncol
    flat = tokens.reshape(grand_total, feature_width).astype(jnp.float32)
    token_average = lax.optimization_barrier(jnp.mean(flat, -1, keepdims=True))
    centered_input = flat - token_average
    inverse_deviation = lax.rsqrt(lax.optimization_barrier(jnp.mean(centered_input * centered_input, -1, keepdims=True)) + EPS)
    standardized_input = centered_input * inverse_deviation
    normalized_tokens = (standardized_input * gain).astype(jnp.bfloat16)
    qkv = jnp.dot(normalized_tokens, w_qkv.reshape(feature_width, 3 * feature_width), preferred_element_type=jnp.float32)
    qkv = qkv.astype(jnp.bfloat16).reshape(nrow, ncol, 3, feature_width)
    rolled = jnp.roll(qkv, (-SHIFT, -SHIFT), (0, 1))
    out_grad = jnp.dot(cotangent.reshape(grand_total, feature_width), w_proj.T, preferred_element_type=jnp.float32)
    out_grad = out_grad.astype(jnp.bfloat16).reshape(nrow, ncol, feature_width)
    rolled_grad = jnp.roll(out_grad, (-SHIFT, -SHIFT), (0, 1))
    onehot = offsets()
    bias = jnp.dot(onehot, rel_table, precision=HIGH).reshape(WIN * WIN, WIN * WIN, HEADS).transpose(2, 0, 1)
    col_lab = region(jnp.arange(ncol, dtype=jnp.int32), ncol)

    def band(index):
        start = index * WIN
        qkv_band = lax.dynamic_slice_in_dim(rolled, start, WIN, 0)
        grad_band = lax.dynamic_slice_in_dim(rolled_grad, start, WIN, 0)
        valid_band = lax.dynamic_slice_in_dim(valid, start, WIN, 0)
        row_lab = region(start + jnp.arange(WIN, dtype=jnp.int32), nrow)
        labels = 3 * row_lab[:, None] + col_lab[None, :]
        return attend(qkv_band, grad_band, labels, valid_band, bias, onehot)
    attended, grads, tparts = lax.map(band, jnp.arange(nrow // WIN, dtype=jnp.int32))
    attended = attended.reshape(nrow, ncol, feature_width)
    grads = grads.reshape(nrow, ncol, 3, feature_width)
    attn_out = jnp.roll(attended, (SHIFT, SHIFT), (0, 1)).reshape(grand_total, feature_width)
    qkv_grad = jnp.roll(grads, (SHIFT, SHIFT), (0, 1))
    group = feature_width // N_HEAD
    branch = jnp.zeros((grand_total, feature_width), jnp.float32)
    norm_grad = jnp.zeros((grand_total, feature_width), jnp.float32)
    for index in range(N_HEAD):
        low = index * group
        part = jnp.dot(attn_out[:, low:low + group], w_proj[low:low + group], preferred_element_type=jnp.float32)
        branch = branch + lax.optimization_barrier(part.astype(jnp.bfloat16)).astype(jnp.float32)
        piece = qkv_grad[:, :, :, low:low + group].reshape(grand_total, 3 * group)
        weights = w_qkv[:, :, low:low + group].reshape(feature_width, 3 * group)
        back = jnp.dot(piece, weights.T, preferred_element_type=jnp.float32)
        norm_grad = norm_grad + lax.optimization_barrier(back.astype(jnp.bfloat16)).astype(jnp.float32)
    mixed = (flat + branch).astype(jnp.bfloat16).reshape(nrow, ncol, feature_width)
    scale = 1.0 / math.sqrt(grand_total)
    proj_grad = jnp.dot(attn_out.T, cotangent.reshape(grand_total, feature_width), preferred_element_type=jnp.float32) * scale
    table_grad = lax.optimization_barrier(jnp.sum(tparts, 0)) * (WIN * scale)
    scaled_tokens = norm_grad * gain
    token_gradient = cotangent.reshape(grand_total, feature_width).astype(jnp.float32) + inverse_deviation * (scaled_tokens - lax.optimization_barrier(jnp.mean(scaled_tokens, -1, keepdims=True)) - standardized_input * lax.optimization_barrier(jnp.mean(scaled_tokens * standardized_input, -1, keepdims=True)))
    token_gradient = token_gradient.astype(jnp.bfloat16).reshape(nrow, ncol, feature_width)
    return (mixed, token_gradient, proj_grad, table_grad)
```

```python
import math

import jax
import jax.numpy as jnp
from jax import lax
from jax.experimental import pallas as pl
from jax.experimental.pallas import tpu as pltpu
from jax.sharding import PartitionSpec as P

HD = 64
WIN = 8
SHIFT = 4
EPS = 1e-05
F32 = jnp.float32
BF16 = jnp.bfloat16
SPAN = 2 * WIN - 1
POS = WIN * WIN


def dot(a, b, ca, cb):
    return lax.dot_general(a, b, (((ca,), (cb,)), ((), ())), preferred_element_type=F32)


def rows_to_table(vectors):
    heads = vectors.shape[0] // 2
    even = vectors[:heads].reshape(heads, 8, 16)
    odd = jnp.concatenate([vectors[heads:, 8:], vectors[heads:, :8]], 1).reshape(heads, 8, 16)
    both = jnp.stack([even, odd], 2).reshape(heads, 16, 16)[:, :SPAN, :SPAN]
    return both.reshape(heads, SPAN * SPAN).T


def table_to_rows(table):
    heads = table.shape[1]
    grid = jnp.pad(table.T.reshape(heads, SPAN, SPAN), ((0, 0), (0, 1), (0, 1)))
    grid = grid.reshape(heads, 8, 2, 16)
    even = grid[:, :, 0].reshape(heads, 128)
    odd = grid[:, :, 1].reshape(heads, 128)
    odd = jnp.concatenate([odd[:, 120:], odd[:, :120]], 1)
    return jnp.concatenate([even, odd], 0)


def attention_kernel(
    flags_ref, x_ref, wq_ref, wp_ref, tab_ref, val_ref, rs_ref, keep_ref, send_ref
):
    channels = wp_ref.shape[0]
    heads = channels // HD
    d = wp_ref.shape[1]
    scale = HD ** (-0.5)
    bands = x_ref.shape[0] // 2
    ncol = x_ref.shape[3]
    wins = ncol // WIN
    rows = 2 * x_ref.shape[2] * ncol
    lanes = heads * POS

    lane128 = lax.broadcasted_iota(jnp.int32, (8, 128), 1)
    even_lane = ((lane128 // 8) % 2) == 0

    tab = tab_ref[...]
    shifted = [pltpu.roll(tab, (b - 7) % 128, 1) for b in range(WIN)]
    per_head = []
    for h in range(heads):
        ev = jnp.concatenate([s[h : h + 1] for s in shifted], 0)
        od = jnp.concatenate([s[heads + h : heads + h + 1] for s in shifted], 0)
        per_head.append(jnp.where(even_lane, ev, od))
    bias_rows = []
    for a in range(WIN):
        pieces = []
        for p in range(heads // 2):
            lo = pltpu.roll(per_head[2 * p], (-(7 - a) * 8) % 128, 1)
            hi = pltpu.roll(per_head[2 * p + 1], (64 - (7 - a) * 8) % 128, 1)
            pieces.append(jnp.where(lane128 < 64, lo, hi))
        bias_rows.append(jnp.concatenate(pieces, 1))
    bias = jnp.concatenate(bias_rows, 0)

    key_pos = lax.broadcasted_iota(jnp.int32, (POS, lanes), 0)
    query_pos = lax.broadcasted_iota(jnp.int32, (POS, lanes), 1) % POS
    same_pos = key_pos == query_pos
    same_row_half = (key_pos // (WIN * SHIFT)) == (query_pos // (WIN * SHIFT))
    same_col_half = ((key_pos // SHIFT) % 2) == ((query_pos // SHIFT) % 2)
    last_row = flags_ref[0] == 1
    last_col = flags_ref[1] == 1
    core = flags_ref[2]

    lane_head = lax.broadcasted_iota(jnp.int32, (POS, channels), 1) // HD
    head_f = [(lane_head == h).astype(F32) for h in range(heads)]
    head_b = [m.astype(BF16) for m in head_f]

    ds_total = jnp.zeros((POS, lanes), F32)
    wt = jnp.zeros((d, channels), F32)
    for w in range(bands):
        xn = x_ref[2 * w : 2 * w + 2, 0].reshape(rows, d)
        ct = x_ref[2 * w : 2 * w + 2, 1].reshape(rows, d)
        qkv = dot(xn, wq_ref[...], 1, 0).reshape(WIN, wins, WIN, 3 * channels)
        dog = dot(ct, wp_ref[...], 1, 1).reshape(WIN, wins, WIN, channels)
        outs, dqs, dks, dvs = [], [], [], []
        for u in range(wins):
            part = qkv[:, u].reshape(POS, 3 * channels).astype(BF16)
            q = part[:, :channels]
            k = part[:, channels : 2 * channels]
            v = part[:, 2 * channels :]
            do = dog[:, u].reshape(POS, channels).astype(BF16)
            qbd = jnp.concatenate([q * m for m in head_b], 0)
            dbd = jnp.concatenate([do * m for m in head_b], 0)
            s = dot(k, qbd, 1, 1) * scale + bias
            valid = val_ref[:, w * wins + u : w * wins + u + 1]
            allowed = same_pos | (jnp.broadcast_to(valid, (POS, lanes)) == 1.0)
            if w == bands - 1:
                allowed = allowed & (same_row_half | jnp.logical_not(last_row))
            if u == wins - 1:
                allowed = allowed & (same_col_half | jnp.logical_not(last_col))
            s = jnp.where(allowed, s, -1e30)
            e = jnp.exp(s - jnp.max(s, 0, keepdims=True))
            p = e / jnp.sum(e, 0, keepdims=True)
            pb = p.astype(BF16)
            dp = dot(v, dbd, 1, 1)
            ds = p * (dp - jnp.sum(p * dp, 0, keepdims=True))
            dsb = ds.astype(BF16)
            ds_total = ds_total + ds
            dvs.append(dot(pb, dbd, 1, 0))
            dks.append(dot(dsb, qbd, 1, 0) * scale)
            o_all = dot(pb, v, 0, 0)
            dq_all = dot(dsb, k, 0, 0)
            o = o_all[:POS] * head_f[0]
            dq = dq_all[:POS] * head_f[0]
            for h in range(1, heads):
                o = o + o_all[h * POS : (h + 1) * POS] * head_f[h]
                dq = dq + dq_all[h * POS : (h + 1) * POS] * head_f[h]
            outs.append(o)
            dqs.append(dq * scale)

        def patches(parts):
            parts = [z.reshape(WIN, 1, WIN, channels) for z in parts]
            return jnp.concatenate(parts, 1).reshape(rows, channels).astype(BF16)

        attn = patches(outs)
        grads = jnp.concatenate([patches(dqs), patches(dks), patches(dvs)], 1)
        shape = (2,) + rs_ref.shape[2:]
        rs_ref[2 * w : 2 * w + 2, 0] = dot(attn, wp_ref[...], 1, 0).astype(BF16).reshape(shape)
        rs_ref[2 * w : 2 * w + 2, 1] = dot(grads, wq_ref[...], 1, 1).astype(BF16).reshape(shape)
        wt = wt + dot(ct, attn, 0, 0)

    halves = wt.reshape(d // 16, 2, 8, channels)
    first = core == 0
    keep_ref[: d // 16] = jnp.where(first, halves[:, 0], halves[:, 1])
    send_ref[: d // 16] = jnp.where(first, halves[:, 1], halves[:, 0])

    diag = [jnp.zeros((8, 128), F32) for _ in range(heads)]
    for a in range(WIN):
        for p in range(heads // 2):
            block = ds_total[8 * a : 8 * a + 8, 128 * p : 128 * p + 128]
            lo = jnp.where(lane128 < 64, block, 0.0)
            hi = jnp.where(lane128 < 64, 0.0, block)
            diag[2 * p] = diag[2 * p] + pltpu.roll(lo, (7 - a) * 8, 1)
            diag[2 * p + 1] = diag[2 * p + 1] + pltpu.roll(hi, ((7 - a) * 8 - 64) % 128, 1)
    evens = [jnp.where(even_lane, t, 0.0) for t in diag]
    odds = [jnp.where(even_lane, 0.0, t) for t in diag]
    total = jnp.zeros((8, 128), F32)
    for b in range(WIN):
        line = jnp.concatenate([t[b : b + 1] for t in evens + odds], 0)
        total = total + pltpu.roll(line, 7 - b, 1)
    both = jnp.concatenate([total, jnp.zeros((8, channels - 128), F32)], 1)
    keep_ref[d // 16] = both
    send_ref[d // 16] = both


def attention(flags, gathered, w_qkv, w_proj, table, valid):
    d = w_proj.shape[1]
    channels = w_proj.shape[0]
    piece = jax.ShapeDtypeStruct((d // 16 + 1, 8, channels), F32)
    vmem = pl.BlockSpec(memory_space=pltpu.VMEM)
    return pl.pallas_call(
        attention_kernel,
        out_shape=(jax.ShapeDtypeStruct(gathered.shape, BF16), piece, piece),
        in_specs=[pl.BlockSpec(memory_space=pltpu.SMEM)] + [vmem] * 5,
        out_specs=(vmem, vmem, vmem),
        compiler_params=pltpu.CompilerParams(vmem_limit_bytes=44 * 1024 * 1024),
        cost_estimate=pl.CostEstimate(
            flops=3_000_000_000, bytes_accessed=9_000_000, transcendentals=131072
        ),
        name="window_attention",
    )(flags, gathered, w_qkv, w_proj, table, valid)


def on_device(tokens, valid, gain, w_qkv, w_proj, rel_table, cotangent):
    part_rows, ncol, d = tokens.shape
    n_head = lax.axis_size("head")
    n_row = lax.axis_size("row")
    n_col = lax.axis_size("col")
    tile_rows = part_rows * n_head
    channels = w_proj.shape[0]
    row = lax.axis_index("row")
    col = lax.axis_index("col")
    head = lax.axis_index("head")

    groups = [
        [r * n_head + h for h in range(1, n_head)] + [(r + 1) % n_row * n_head]
        for r in range(n_row)
    ]
    left = [(c, (c - 1) % n_col) for c in range(n_col)]
    right = [(c, (c + 1) % n_col) for c in range(n_col)]

    strips = jnp.stack([tokens[:, :SHIFT], cotangent[:, :SHIFT]])
    strips = lax.ppermute(strips, "col", left)
    down = [(r * n_head, (r + 1) % n_row * n_head) for r in range(n_row)]
    val = valid.astype(F32).reshape(tile_rows // WIN, WIN, ncol // WIN, WIN)
    val = val.transpose(1, 3, 0, 2).reshape(POS, -1)
    val = jnp.where(head == 0, lax.ppermute(val, ("row", "head"), down), val)

    moved = jnp.concatenate([tokens[:, SHIFT:], strips[0]], 1).astype(F32)
    mean = jnp.mean(moved, -1, keepdims=True)
    centered = moved - mean
    rstd = lax.rsqrt(jnp.mean(centered * centered, -1, keepdims=True) + EPS)
    normed = (centered * rstd * gain).astype(BF16)
    moved_grad = jnp.concatenate([cotangent[:, SHIFT:], strips[1]], 1)
    packet = jnp.stack([normed, moved_grad])
    packet = jnp.broadcast_to(packet[None], (n_head,) + packet.shape)
    gathered = lax.all_to_all(
        packet, ("row", "head"), 0, 0, axis_index_groups=groups, tiled=True
    )

    tile = jnp.where(head == 0, (row + n_row - 1) % n_row, row)
    flags = jnp.stack([tile == n_row - 1, col == n_col - 1, col % 2 == 1]).astype(jnp.int32)
    terms, keep, send = attention(
        flags, gathered, w_qkv.reshape(d, 3 * channels), w_proj, table_to_rows(rel_table), val
    )

    swap = [(c, c ^ 1) for c in range(n_col)]
    got = lax.ppermute(send, "col", swap)
    shares = lax.all_to_all(terms, ("row", "head"), 0, 0, axis_index_groups=groups, tiled=True)
    summed = jnp.sum(shares.astype(F32), 0)
    edge = lax.ppermute(summed[:, :, -SHIFT:].astype(BF16), "col", right).astype(F32)
    summed = jnp.concatenate([edge, summed[:, :, :-SHIFT]], 2)

    pair = keep + got
    pieces = pair[:-1].astype(BF16)
    table_part = pair[-1, :, :128]
    table_hi = table_part.astype(BF16)
    table_lo = (table_part - table_hi.astype(F32)).astype(BF16)
    table_part = jnp.concatenate([table_hi, table_lo], 1)
    table_part = jnp.broadcast_to(table_part[None], (pieces.shape[0],) + table_part.shape)
    pieces = jnp.concatenate([pieces, table_part], 1)
    cores = [
        [r * n_col + c for r in range(n_row) for c in range(n_col) if c % 2 == parity]
        for parity in range(2)
    ]
    pieces = lax.all_to_all(pieces, ("row", "col"), 0, 0, axis_index_groups=cores, tiled=True)
    pieces = jnp.sum(pieces.astype(F32), 0)
    scale = 1.0 / math.sqrt(tile_rows * ncol * n_row * n_col)
    proj_grad = pieces[:8].T * scale
    table_grad = rows_to_table(pieces[8:, :128] + pieces[8:, 128:]) * (WIN * scale)

    flat = tokens.astype(F32)
    mean = jnp.mean(flat, -1, keepdims=True)
    centered = flat - mean
    rstd = lax.rsqrt(jnp.mean(centered * centered, -1, keepdims=True) + EPS)
    xhat = centered * rstd
    mixed = (flat + summed[0]).astype(BF16)
    scaled = summed[1] * gain
    token_gradient = cotangent.astype(F32) + rstd * (
        scaled
        - jnp.mean(scaled, -1, keepdims=True)
        - xhat * jnp.mean(scaled * xhat, -1, keepdims=True)
    )
    return (mixed, token_gradient.astype(BF16), proj_grad, table_grad)


def solution(mesh):
    return jax.shard_map(
        on_device,
        mesh=mesh,
        in_specs=(
            P(("row", "head"), "col", None),
            P("row", "col"),
            P(),
            P(None, None, "head"),
            P("head", None),
            P(None, "head"),
            P(("row", "head"), "col", None),
        ),
        out_specs=(
            P(("row", "head"), "col", None),
            P(("row", "head"), "col", None),
            P("head", ("row", "col")),
            P(None, "head"),
        ),
        check_vma=False,
    )
```

```python
import math

import jax
import jax.numpy as jnp
from jax import lax
from jax.experimental import pallas as pl
from jax.experimental.pallas import tpu as pltpu
from jax.sharding import PartitionSpec as P

HD = 64
WIN = 8
SHIFT = 4
EPS = 1e-05
F32 = jnp.float32
BF16 = jnp.bfloat16
SPAN = 2 * WIN - 1
POS = WIN * WIN
VMEM_LIMIT = 56 * 1024 * 1024


def dot(a, b, ca, cb):
    return lax.dot_general(a, b, (((ca,), (cb,)), ((), ())), preferred_element_type=F32)


def rows_to_table(vectors):
    heads = vectors.shape[0] // 2
    even = vectors[:heads].reshape(heads, 8, 16)
    odd = jnp.concatenate([vectors[heads:, 8:], vectors[heads:, :8]], 1).reshape(heads, 8, 16)
    both = jnp.stack([even, odd], 2).reshape(heads, 16, 16)[:, :SPAN, :SPAN]
    return both.reshape(heads, SPAN * SPAN).T


def table_to_rows(table):
    heads = table.shape[1]
    grid = jnp.pad(table.T.reshape(heads, SPAN, SPAN), ((0, 0), (0, 1), (0, 1)))
    grid = grid.reshape(heads, 8, 2, 16)
    even = grid[:, :, 0].reshape(heads, 128)
    odd = grid[:, :, 1].reshape(heads, 128)
    odd = jnp.concatenate([odd[:, 120:], odd[:, :120]], 1)
    return jnp.concatenate([even, odd], 0)


def attention_kernel(
    flags_ref, x1, x2, x3, x4, c1, c2, c3, c4, wq_in, wp_in, tab_ref,
    o1, o2, o3, o4, keep_ref, send_ref,
    xs_ref, cs_ref, wq_ref, wp_ref, out_ref, grad_cols, attn_cols, attn_edge, sems,
):
    channels = wp_ref.shape[0]
    heads = channels // HD
    d = wp_ref.shape[1]
    scale = HD ** (-0.5)
    parts = cs_ref.shape[0]
    ncol = grad_cols.shape[1] - WIN
    wins = ncol // WIN
    own = cs_ref.shape[1]
    prow = own // ncol
    strip = prow * SHIFT
    bands = parts * prow // WIN
    rows = own * parts // bands
    lanes = heads * POS
    head = flags_ref[3]
    slots = []
    for k in range(parts):
        slot = SLOTS[0][k]
        for h in range(1, parts):
            slot = jnp.where(head == h, SLOTS[h][k], slot)
        slots.append(slot)
    moves = [(wp_in, wp_ref), (wq_in, wq_ref)]
    moves += [(c, cs_ref.at[slot]) for slot, c in zip(slots, (c1, c2, c3, c4))]
    moves += [(x, xs_ref.at[slot]) for slot, x in zip(slots, (x1, x2, x3, x4))]
    moves = [pltpu.make_async_copy(a, b, sems.at[i]) for i, (a, b) in enumerate(moves)]
    for move in moves:
        move.start()

    lane128 = lax.broadcasted_iota(jnp.int32, (8, 128), 1)
    even_lane = ((lane128 // 8) % 2) == 0

    tab = tab_ref[...]
    shifted = [pltpu.roll(tab, (b - 7) % 128, 1) for b in range(WIN)]
    per_head = []
    for h in range(heads):
        ev = jnp.concatenate([s[h : h + 1] for s in shifted], 0)
        od = jnp.concatenate([s[heads + h : heads + h + 1] for s in shifted], 0)
        per_head.append(jnp.where(even_lane, ev, od))
    bias_rows = []
    for a in range(WIN):
        pieces = []
        for p in range(heads // 2):
            lo = pltpu.roll(per_head[2 * p], (-(7 - a) * 8) % 128, 1)
            hi = pltpu.roll(per_head[2 * p + 1], (64 - (7 - a) * 8) % 128, 1)
            pieces.append(jnp.where(lane128 < 64, lo, hi))
        bias_rows.append(jnp.concatenate(pieces, 1))
    bias = jnp.concatenate(bias_rows, 0)

    key_pos = lax.broadcasted_iota(jnp.int32, (POS, lanes), 0)
    query_pos = lax.broadcasted_iota(jnp.int32, (POS, lanes), 1) % POS
    same_pos = key_pos == query_pos
    same_row_half = (key_pos // (WIN * SHIFT)) == (query_pos // (WIN * SHIFT))
    same_col_half = ((key_pos // SHIFT) % 2) == ((query_pos // SHIFT) % 2)
    last_row = flags_ref[0] == 1
    last_col = flags_ref[1] == 1
    core = flags_ref[2]

    lane_head = lax.broadcasted_iota(jnp.int32, (POS, channels), 1) // HD
    head_f = [(lane_head == h).astype(F32) for h in range(heads)]
    head_b = [m.astype(BF16) for m in head_f]

    for move in moves:
        move.wait()

    edge = jnp.concatenate([xs_ref[x, own : own + strip] for x in range(parts)], 0)
    edge_grad = dot(edge, wp_ref[...], 1, 1)
    attn_edge[...] = edge_grad

    results = [
        pltpu.make_async_copy(out_ref.at[slot], out, sems.at[len(moves) + k])
        for k, (slot, out) in enumerate(zip(slots, (o1, o2, o3, o4)))
    ]
    ds_total = jnp.zeros((POS, lanes), F32)
    wt = jnp.zeros((d, channels), F32)
    per_band = parts // bands
    for w in range(bands):
        members = range(w * per_band, (w + 1) * per_band)
        xn = jnp.concatenate([xs_ref[x, :own] for x in members], 0)
        ct = jnp.concatenate([cs_ref[x] for x in members], 0)
        queries, keys, values = [
            dot(xn, wq_ref[t], 1, 0).reshape(WIN, wins, WIN, channels) for t in range(3)
        ]
        marks = xs_ref[w * per_band, own + strip :]
        key_row = lax.broadcasted_iota(jnp.int32, (POS, marks.shape[0]), 0) // WIN + w * WIN
        tile_row = lax.broadcasted_iota(jnp.int32, (POS, marks.shape[0]), 1)
        marks = dot((key_row == tile_row).astype(BF16), marks[:, :128], 1, 0)
        key_col = lax.broadcasted_iota(jnp.int32, marks.shape, 0) % WIN
        tile_col = lax.broadcasted_iota(jnp.int32, marks.shape, 1)
        grad_cols[:, :ncol] = dot(ct, wp_ref[...], 1, 1).reshape(WIN, ncol, channels)
        for i in range(WIN):
            at = (w * WIN + i) * SHIFT
            grad_cols[i, ncol : ncol + SHIFT] = attn_edge[at : at + SHIFT]
        dog = grad_cols[:, SHIFT : SHIFT + ncol].reshape(WIN, wins, WIN, channels)
        outs, dqs, dks, dvs = [], [], [], []
        for u in range(wins):
            q = queries[:, u].reshape(POS, channels).astype(BF16)
            k = keys[:, u].reshape(POS, channels).astype(BF16)
            v = values[:, u].reshape(POS, channels).astype(BF16)
            do = dog[:, u].reshape(POS, channels).astype(BF16)
            qbd = jnp.concatenate([q * m for m in head_b], 0)
            dbd = jnp.concatenate([do * m for m in head_b], 0)
            s = dot(k, qbd, 1, 1) * scale + bias
            valid = jnp.where(tile_col == key_col + u * WIN, marks, 0.0)
            valid = jnp.sum(valid, 1, keepdims=True)
            allowed = same_pos | (jnp.broadcast_to(valid, (POS, lanes)) == 1.0)
            if w == bands - 1:
                allowed = allowed & (same_row_half | jnp.logical_not(last_row))
            if u == wins - 1:
                allowed = allowed & (same_col_half | jnp.logical_not(last_col))
            s = jnp.where(allowed, s, -1e30)
            e = jnp.exp(s - jnp.max(s, 0, keepdims=True))
            p = e / jnp.sum(e, 0, keepdims=True)
            pb = p.astype(BF16)
            dp = dot(v, dbd, 1, 1)
            ds = p * (dp - jnp.sum(p * dp, 0, keepdims=True))
            dsb = ds.astype(BF16)
            ds_total = ds_total + ds
            dvs.append(dot(pb, dbd, 1, 0))
            dks.append(dot(dsb, qbd, 1, 0) * scale)
            o_all = dot(pb, v, 0, 0)
            dq_all = dot(dsb, k, 0, 0)
            o = o_all[:POS] * head_f[0]
            dq = dq_all[:POS] * head_f[0]
            for h in range(1, heads):
                o = o + o_all[h * POS : (h + 1) * POS] * head_f[h]
                dq = dq + dq_all[h * POS : (h + 1) * POS] * head_f[h]
            outs.append(o)
            dqs.append(dq * scale)

        def patches(pieces):
            pieces = [z.reshape(WIN, 1, WIN, channels) for z in pieces]
            return jnp.concatenate(pieces, 1).reshape(rows, channels)

        attn = patches(outs)
        back = dot(patches(dqs).astype(BF16), wq_ref[0], 1, 1)
        back = back + dot(patches(dks).astype(BF16), wq_ref[1], 1, 1)
        back = (back + dot(patches(dvs).astype(BF16), wq_ref[2], 1, 1)).astype(BF16)
        branch = dot(attn.astype(BF16), wp_ref[...], 1, 0).astype(BF16)
        for i, x in enumerate(members):
            out_ref[x, :own] = back[i * own : (i + 1) * own]
            out_ref[x, own:] = branch[i * own : (i + 1) * own]
        for slot, result in zip(slots, results):

            @pl.when(slot // per_band == w)
            def _(result=result):
                result.start()

        attn_cols[:, :SHIFT] = jnp.zeros((WIN, SHIFT, channels), F32)
        attn_cols[:, SHIFT : SHIFT + ncol] = attn.reshape(WIN, ncol, channels)
        for i in range(WIN):
            at = (w * WIN + i) * SHIFT
            attn_edge[at : at + SHIFT] = attn_cols[i, ncol : ncol + SHIFT]
        wt = wt + dot(ct, attn_cols[:, :ncol].reshape(rows, channels).astype(BF16), 0, 0)

    wt = wt + dot(edge, attn_edge[...].astype(BF16), 0, 0)
    halves = wt.reshape(d // 16, 2, 8, channels)
    first = core == 0
    keep_ref[: d // 16] = jnp.where(first, halves[:, 0], halves[:, 1])
    send_ref[: d // 16] = jnp.where(first, halves[:, 1], halves[:, 0])

    diag = [jnp.zeros((8, 128), F32) for _ in range(heads)]
    for a in range(WIN):
        for p in range(heads // 2):
            block = ds_total[8 * a : 8 * a + 8, 128 * p : 128 * p + 128]
            lo = jnp.where(lane128 < 64, block, 0.0)
            hi = jnp.where(lane128 < 64, 0.0, block)
            diag[2 * p] = diag[2 * p] + pltpu.roll(lo, (7 - a) * 8, 1)
            diag[2 * p + 1] = diag[2 * p + 1] + pltpu.roll(hi, ((7 - a) * 8 - 64) % 128, 1)
    evens = [jnp.where(even_lane, t, 0.0) for t in diag]
    odds = [jnp.where(even_lane, 0.0, t) for t in diag]
    total = jnp.zeros((8, 128), F32)
    for b in range(WIN):
        line = jnp.concatenate([t[b : b + 1] for t in evens + odds], 0)
        total = total + pltpu.roll(line, 7 - b, 1)
    both = jnp.concatenate([total, jnp.zeros((8, channels - 128), F32)], 1)
    keep_ref[d // 16] = both
    send_ref[d // 16] = both
    for result in results:
        result.wait()


def attention(ncol, flags, normed, grads, w_qkv, w_proj, table):
    channels, d = w_proj.shape
    parts = len(grads)
    own = grads[0].shape[0]
    prow = own // ncol
    piece = jax.ShapeDtypeStruct((d // 16 + 1, 8, channels), F32)
    term = jax.ShapeDtypeStruct((2 * own, d), BF16)
    vmem = pl.BlockSpec(memory_space=pltpu.VMEM)
    return pl.pallas_call(
        attention_kernel,
        out_shape=(term,) * parts + (piece, piece),
        in_specs=[pl.BlockSpec(memory_space=pltpu.SMEM)]
        + [pl.BlockSpec(memory_space=pltpu.HBM)] * (2 * parts + 2)
        + [vmem],
        out_specs=(pl.BlockSpec(memory_space=pltpu.HBM),) * parts + (vmem, vmem),
        scratch_shapes=[
            pltpu.VMEM((parts,) + normed[0].shape, BF16),
            pltpu.VMEM((parts,) + grads[0].shape, BF16),
            pltpu.VMEM(w_qkv.shape, BF16),
            pltpu.VMEM(w_proj.shape, BF16),
            pltpu.VMEM((parts, 2 * own, d), BF16),
            pltpu.VMEM((WIN, ncol + WIN, channels), F32),
            pltpu.VMEM((WIN, ncol + WIN, channels), F32),
            pltpu.VMEM((parts * prow * SHIFT, channels), F32),
            pltpu.SemaphoreType.DMA((3 * parts + 2,)),
        ],
        compiler_params=pltpu.CompilerParams(vmem_limit_bytes=VMEM_LIMIT),
        cost_estimate=pl.CostEstimate(
            flops=3_000_000_000, bytes_accessed=9_000_000, transcendentals=131072
        ),
        name="window_attention",
    )(flags, *normed, *grads, w_qkv, w_proj, table)


def strips_kernel(tokens_ref, grads_ref, out_ref):
    out_ref[...] = jnp.concatenate([tokens_ref[:, :SHIFT], grads_ref[:, :SHIFT]], 1)


def left_strips(tokens, grads):
    prow, ncol, d = tokens.shape
    spec = pl.BlockSpec((prow, 16, d), lambda i: (0, 0, 0))
    return pl.pallas_call(
        strips_kernel,
        grid=(1,),
        out_shape=jax.ShapeDtypeStruct((prow, 2 * SHIFT, d), BF16),
        in_specs=[spec, spec],
        out_specs=pl.BlockSpec((prow, 2 * SHIFT, d), lambda i: (0, 0, 0)),
        compiler_params=pltpu.CompilerParams(vmem_limit_bytes=VMEM_LIMIT),
        cost_estimate=pl.CostEstimate(flops=0, bytes_accessed=300_000, transcendentals=0),
        name="left_strips",
    )(tokens, grads)


def norm_kernel(tokens_ref, strips_ref, gain_ref, valid_ref, out_ref, cols, strip_rows):
    prow, ncol, d = tokens_ref.shape
    own = prow * ncol
    strip = prow * SHIFT
    cols[:, :ncol] = tokens_ref[...].astype(F32)
    for i in range(prow):
        both = strips_ref[i].astype(F32)
        cols[i, ncol : ncol + SHIFT] = both[:SHIFT]
        strip_rows[i * SHIFT : (i + 1) * SHIFT] = both[SHIFT:]
    x = cols[:, SHIFT : SHIFT + ncol].reshape(own, d)
    x = x - jnp.mean(x, -1, keepdims=True)
    rstd = lax.rsqrt(jnp.mean(x * x, -1, keepdims=True) + EPS)
    out_ref[:own] = (x * rstd * gain_ref[...]).astype(BF16)
    out_ref[own : own + strip] = strip_rows[...].astype(BF16)
    out_ref[own + strip :] = jnp.zeros((valid_ref.shape[0], d), BF16)
    out_ref[own + strip :, :ncol] = valid_ref[...].astype(F32).astype(BF16)


def norm(tokens, strips, gain, valid):
    prow, ncol, d = tokens.shape
    strip = prow * SHIFT
    vmem = pl.BlockSpec(memory_space=pltpu.VMEM)
    return pl.pallas_call(
        norm_kernel,
        out_shape=jax.ShapeDtypeStruct((prow * ncol + strip + valid.shape[0], d), BF16),
        in_specs=[vmem] * 4,
        out_specs=vmem,
        scratch_shapes=[pltpu.VMEM((prow, ncol + WIN, d), F32), pltpu.VMEM((strip, d), F32)],
        compiler_params=pltpu.CompilerParams(vmem_limit_bytes=VMEM_LIMIT),
        cost_estimate=pl.CostEstimate(
            flops=1_500_000, bytes_accessed=600_000, transcendentals=128
        ),
        name="layer_norm",
    )(tokens, strips, gain, valid)


ROUTES = (
    ((0, 3), (0, 0), (0, 1), (1, 2)),
    ((-1, 1), (0, 2), (0, 3), (0, 0)),
    ((0, 2), (0, 3), (0, 0), (0, 1)),
    ((-1, 0), (0, 1), (0, 2), (1, 3)),
)
SLOTS = ((0, 2, 1, 3), (1, 3, 2, 0), (2, 0, 3, 1), (3, 1, 0, 2))


def on_device(tokens, valid, gain, w_qkv, w_proj, rel_table, cotangent):
    part_rows, ncol, d = tokens.shape
    n_head = lax.axis_size("head")
    n_row = lax.axis_size("row")
    n_col = lax.axis_size("col")
    tile_rows = part_rows * n_head
    own = part_rows * ncol
    strip = part_rows * SHIFT
    channels = w_proj.shape[0]
    row = lax.axis_index("row")
    col = lax.axis_index("col")
    head = lax.axis_index("head")

    left = [(c, (c - 1) % n_col) for c in range(n_col)]
    right = [(c, (c + 1) % n_col) for c in range(n_col)]
    swap = [(c, c ^ 1) for c in range(n_col)]
    routes = [
        [
            (r * n_head + x, (r + step) % n_row * n_head + h)
            for r in range(n_row)
            for x, (step, h) in enumerate(route)
        ]
        for route in ROUTES
    ]
    returns = [[(b, a) for a, b in route] for route in routes]

    def send(value, route):
        return lax.ppermute(value, ("row", "head"), route)

    strips = left_strips(tokens, cotangent)
    sent, _ = lax.optimization_barrier((cotangent, strips))
    strips = lax.ppermute(strips, "col", left)
    grads = [send(sent.reshape(own, d), route) for route in routes]

    normed = norm(tokens, strips, gain[None], valid)
    normed = [send(normed, route) for route in routes]

    last = jnp.where(head >= 2, row == 0, row == n_row - 1)
    flags = [last.astype(jnp.int32), (col == n_col - 1).astype(jnp.int32), col % 2, head]
    flags = jnp.stack(flags)
    outs = attention(
        ncol,
        flags,
        normed,
        grads,
        w_qkv.transpose(1, 0, 2),
        w_proj,
        table_to_rows(rel_table),
    )
    terms = [send(part, route) for part, route in zip(outs[:n_head], returns)]

    pair = outs[-2] + lax.ppermute(outs[-1], "col", swap)
    table_part = jnp.broadcast_to(pair[-1:, :, :128], (d // 16, 8, 128))
    pieces = jnp.concatenate([pair[:-1], table_part], 2).astype(BF16)
    cores = [
        [r * n_col + c for r in range(n_row) for c in range(n_col) if c % 2 == parity]
        for parity in range(2)
    ]
    _, *terms = lax.optimization_barrier((pieces, *terms))
    pieces = lax.all_to_all(pieces, ("row", "col"), 0, 0, axis_index_groups=cores, tiled=True)
    pieces = jnp.sum(pieces.astype(F32), 0)
    scale = 1.0 / math.sqrt(tile_rows * ncol * n_row * n_col)
    proj_grad = pieces[:, :channels].T * scale
    table_grad = rows_to_table(pieces[:, channels:]) * (WIN * scale)

    total = sum(part.astype(F32) for part in terms).reshape(2, part_rows, ncol, d)
    edges = lax.ppermute(total[:, :, -SHIFT:].astype(BF16), "col", right).astype(F32)
    total = jnp.concatenate([edges, total[:, :, :-SHIFT]], 2)
    norm_grad = total[0]

    flat = tokens.astype(F32)
    mean = jnp.mean(flat, -1, keepdims=True)
    centered = flat - mean
    rstd = lax.rsqrt(jnp.mean(centered * centered, -1, keepdims=True) + EPS)
    xhat = centered * rstd
    scaled = norm_grad * gain
    token_gradient = cotangent.astype(F32) + rstd * (
        scaled
        - jnp.mean(scaled, -1, keepdims=True)
        - xhat * jnp.mean(scaled * xhat, -1, keepdims=True)
    )

    mixed = (flat + total[1]).astype(BF16)
    return (mixed, token_gradient.astype(BF16), proj_grad, table_grad)


def solution(mesh):
    return jax.shard_map(
        on_device,
        mesh=mesh,
        in_specs=(
            P(("row", "head"), "col", None),
            P("row", "col"),
            P(),
            P(None, None, "head"),
            P("head", None),
            P(None, "head"),
            P(("row", "head"), "col", None),
        ),
        out_specs=(
            P(("row", "head"), "col", None),
            P(("row", "head"), "col", None),
            P("head", ("row", "col")),
            P(None, "head"),
        ),
        check_vma=False,
    )
```

```python
import math

import jax
import jax.numpy as jnp
from jax import lax
from jax.experimental import pallas as pl
from jax.experimental.pallas import tpu as pltpu
from jax.sharding import PartitionSpec as P

HD = 64
WIN = 8
SHIFT = 4
EPS = 1e-05
F32 = jnp.float32
BF16 = jnp.bfloat16
SPAN = 2 * WIN - 1
POS = WIN * WIN
VMEM_LIMIT = 56 * 1024 * 1024


def dot(a, b, ca, cb):
    return lax.dot_general(a, b, (((ca,), (cb,)), ((), ())), preferred_element_type=F32)


def rows_to_table(vectors):
    heads = vectors.shape[0] // 2
    even = vectors[:heads].reshape(heads, 8, 16)
    odd = jnp.concatenate([vectors[heads:, 8:], vectors[heads:, :8]], 1).reshape(heads, 8, 16)
    both = jnp.stack([even, odd], 2).reshape(heads, 16, 16)[:, :SPAN, :SPAN]
    return both.reshape(heads, SPAN * SPAN).T


def table_to_rows(table):
    heads, count = table.shape
    table = jnp.concatenate([table, jnp.zeros((heads, 256 - count), F32)], 1)
    table = jnp.concatenate([table, table], 0)
    lane = lax.broadcasted_iota(jnp.int32, (2 * heads, 128), 1)
    odd = lax.broadcasted_iota(jnp.int32, (2 * heads, 128), 0) >= heads
    rows = jnp.zeros((2 * heads, 128), F32)
    for a in range(SPAN):
        moved = pltpu.roll(table, (-a * (SPAN - 8)) % 256, 1)[:, :128]
        here = (lane >= 8 * a) & (lane < 8 * a + SPAN) & (odd == (a % 2 == 1))
        rows = jnp.where(here, moved, rows)
    return rows


def attention_kernel(
    flags_ref, x_own, x_other, wq_in, wp_in, half_in, other_half_in, tab_ref,
    own_out, other_out, keep_ref, send_ref,
    xs_ref, wq_all, wp_all, sum_ref, out_ref, grad_cols, attn_cols, attn_edge, tab_parts, sems,
):
    groups, channels, d = wp_all.shape
    heads = channels // HD
    scale = HD ** (-0.5)
    parts = xs_ref.shape[0]
    ncol = grad_cols.shape[1] - WIN
    own = WIN // parts * ncol
    wins = ncol // WIN
    strip = own // ncol * SHIFT
    rows = own * parts
    lanes = heads * POS
    last_row = flags_ref[0] == 1
    last_col = flags_ref[1] == 1
    core = flags_ref[2]
    own_slot = flags_ref[3]
    band = flags_ref[4]

    half = d // 2
    tall = channels // 2
    moves = [
        (x_own, xs_ref.at[own_slot]),
        (x_other, xs_ref.at[1 - own_slot]),
        (wp_in, wp_all.at[0]),
        (wq_in, wq_all.at[0]),
    ]
    first_moves = len(moves)
    for source, at in ((half_in, core), (other_half_in, 1 - core)):
        rows_at = pl.ds(pl.multiple_of(at * half, half), half)
        for t in range(3):
            piece = source.at[t * half : (t + 1) * half, :]
            moves.append((piece, wq_all.at[1, t, rows_at, :]))
        rows_at = pl.ds(pl.multiple_of(at * tall, tall), tall)
        for j in range(d // channels):
            piece = source.at[3 * half + j * tall : 3 * half + (j + 1) * tall, :]
            cols = slice(j * channels, (j + 1) * channels)
            moves.append((piece, wp_all.at[1, rows_at, cols]))
    moves.append((half_in.at[half_in.shape[0] - 16 :, :], tab_parts))
    moves = [pltpu.make_async_copy(a, b, sems.at[i]) for i, (a, b) in enumerate(moves)]
    for move in moves:
        move.start()

    lane128 = lax.broadcasted_iota(jnp.int32, (8, 128), 1)
    even_lane = ((lane128 // 8) % 2) == 0

    def bias_of(tab):
        shifted = [pltpu.roll(tab, (b - 7) % 128, 1) for b in range(WIN)]
        per_head = []
        for h in range(heads):
            ev = jnp.concatenate([s[h : h + 1] for s in shifted], 0)
            od = jnp.concatenate([s[heads + h : heads + h + 1] for s in shifted], 0)
            per_head.append(jnp.where(even_lane, ev, od))
        bias_rows = []
        for a in range(WIN):
            pieces = []
            for p in range(heads // 2):
                lo = pltpu.roll(per_head[2 * p], (-(7 - a) * 8) % 128, 1)
                hi = pltpu.roll(per_head[2 * p + 1], (64 - (7 - a) * 8) % 128, 1)
                pieces.append(jnp.where(lane128 < 64, lo, hi))
            bias_rows.append(jnp.concatenate(pieces, 1))
        return jnp.concatenate(bias_rows, 0)

    key_pos = lax.broadcasted_iota(jnp.int32, (POS, lanes), 0)
    query_pos = lax.broadcasted_iota(jnp.int32, (POS, lanes), 1) % POS
    same_pos = key_pos == query_pos
    same_row_half = (key_pos // (WIN * SHIFT)) == (query_pos // (WIN * SHIFT))
    same_col_half = ((key_pos // SHIFT) % 2) == ((query_pos // SHIFT) % 2)
    lane_head = lax.broadcasted_iota(jnp.int32, (POS, channels), 1) // HD
    head_f = [(lane_head == h).astype(F32) for h in range(heads)]
    head_b = [m.astype(BF16) for m in head_f]

    results = [
        pltpu.make_async_copy(out_ref.at[own_slot], own_out, sems.at[len(moves)]),
        pltpu.make_async_copy(out_ref.at[1 - own_slot], other_out, sems.at[len(moves) + 1]),
    ]

    def group(g):
        if g == 0:
            bias = bias_of(table_to_rows(tab_ref[...]))
        for move in moves[:first_moves] if g == 0 else moves[first_moves:]:
            move.wait()
        if g == 1:
            terms = tab_parts[...].astype(F32)
            bias = bias_of(terms[:8, :128] + terms[:8, 128:256] + terms[8:, :128])
        wp = wp_all[g]

        edge = jnp.concatenate([xs_ref[x, 2 * own : 2 * own + strip] for x in range(parts)], 0)
        edge_grad = dot(edge, wp, 1, 1)
        attn_edge[...] = edge_grad

        ds_total = jnp.zeros((POS, lanes), F32)
        xn = xs_ref[:, :own].reshape(rows, d)
        ct = xs_ref[:, own : 2 * own].reshape(rows, d)
        queries, keys, values = [
            dot(xn, wq_all[g, t], 1, 0).reshape(WIN, wins, WIN, channels) for t in range(3)
        ]
        marks = xs_ref[0, 2 * own + strip :]
        key_row = lax.broadcasted_iota(jnp.int32, (POS, marks.shape[0]), 0) // WIN + band * WIN
        tile_row = lax.broadcasted_iota(jnp.int32, (POS, marks.shape[0]), 1)
        marks = dot((key_row == tile_row).astype(BF16), marks[:, :128], 1, 0)
        key_col = lax.broadcasted_iota(jnp.int32, marks.shape, 0) % WIN
        tile_col = lax.broadcasted_iota(jnp.int32, marks.shape, 1)
        grad_cols[:, :ncol] = dot(ct, wp, 1, 1).reshape(WIN, ncol, channels)
        for i in range(WIN):
            grad_cols[i, ncol : ncol + SHIFT] = attn_edge[i * SHIFT : (i + 1) * SHIFT]
        dog = grad_cols[:, SHIFT : SHIFT + ncol].reshape(WIN, wins, WIN, channels)
        outs, dqs, dks, dvs = [], [], [], []
        for u in range(wins):
            q = queries[:, u].reshape(POS, channels).astype(BF16)
            k = keys[:, u].reshape(POS, channels).astype(BF16)
            v = values[:, u].reshape(POS, channels).astype(BF16)
            do = dog[:, u].reshape(POS, channels).astype(BF16)
            qbd = jnp.concatenate([q * m for m in head_b], 0)
            dbd = jnp.concatenate([do * m for m in head_b], 0)
            s = dot(k, qbd, 1, 1) * scale + bias
            valid = jnp.where(tile_col == key_col + u * WIN, marks, 0.0)
            valid = jnp.sum(valid, 1, keepdims=True)
            allowed = same_pos | (jnp.broadcast_to(valid, (POS, lanes)) == 1.0)
            allowed = allowed & (same_row_half | jnp.logical_not(last_row))
            if u == wins - 1:
                allowed = allowed & (same_col_half | jnp.logical_not(last_col))
            s = jnp.where(allowed, s, -1e30)
            e = jnp.exp(s - jnp.max(s, 0, keepdims=True))
            p = e / jnp.sum(e, 0, keepdims=True)
            pb = p.astype(BF16)
            dp = dot(v, dbd, 1, 1)
            ds = p * (dp - jnp.sum(p * dp, 0, keepdims=True))
            dsb = ds.astype(BF16)
            ds_total = ds_total + ds
            dvs.append(dot(pb, dbd, 1, 0))
            dks.append(dot(dsb, qbd, 1, 0) * scale)
            o_all = dot(pb, v, 0, 0)
            dq_all = dot(dsb, k, 0, 0)
            o = o_all[:POS] * head_f[0]
            dq = dq_all[:POS] * head_f[0]
            for h in range(1, heads):
                o = o + o_all[h * POS : (h + 1) * POS] * head_f[h]
                dq = dq + dq_all[h * POS : (h + 1) * POS] * head_f[h]
            outs.append(o)
            dqs.append(dq * scale)

        def patches(pieces):
            pieces = [z.reshape(WIN, 1, WIN, channels) for z in pieces]
            return jnp.concatenate(pieces, 1).reshape(rows, channels)

        attn = patches(outs)
        back = dot(patches(dqs).astype(BF16), wq_all[g, 0], 1, 1)
        back = back + dot(patches(dks).astype(BF16), wq_all[g, 1], 1, 1)
        back = back + dot(patches(dvs).astype(BF16), wq_all[g, 2], 1, 1)
        branch = dot(attn.astype(BF16), wp, 1, 0)
        for j, term in enumerate((back, branch)):
            term = term.reshape(parts, own, d)
            at = slice(j * own, (j + 1) * own)
            if g < groups - 1:
                sum_ref[:, at] = term
            else:
                out_ref[:, at] = (sum_ref[:, at] + term).astype(BF16)
        if g == groups - 1:
            for result in results:
                result.start()
        attn_cols[:, :SHIFT] = jnp.zeros((WIN, SHIFT, channels), F32)
        attn_cols[:, SHIFT : SHIFT + ncol] = attn.reshape(WIN, ncol, channels)
        for i in range(WIN):
            attn_edge[i * SHIFT : (i + 1) * SHIFT] = attn_cols[i, ncol : ncol + SHIFT]
        wt = dot(ct, attn_cols[:, :ncol].reshape(rows, channels).astype(BF16), 0, 0)
        wt = wt + dot(edge, attn_edge[...].astype(BF16), 0, 0)
        halves = wt.reshape(d // 16, 2, 8, channels)
        first = core == 0
        keep_ref[g, : d // 16] = jnp.where(first, halves[:, 0], halves[:, 1])
        send_ref[g, : d // 16] = jnp.where(first, halves[:, 1], halves[:, 0])

        diag = [jnp.zeros((8, 128), F32) for _ in range(heads)]
        for a in range(WIN):
            for p in range(heads // 2):
                block = ds_total[8 * a : 8 * a + 8, 128 * p : 128 * p + 128]
                lo = jnp.where(lane128 < 64, block, 0.0)
                hi = jnp.where(lane128 < 64, 0.0, block)
                diag[2 * p] = diag[2 * p] + pltpu.roll(lo, (7 - a) * 8, 1)
                diag[2 * p + 1] = diag[2 * p + 1] + pltpu.roll(hi, ((7 - a) * 8 - 64) % 128, 1)
        evens = [jnp.where(even_lane, t, 0.0) for t in diag]
        odds = [jnp.where(even_lane, 0.0, t) for t in diag]
        total = jnp.zeros((8, 128), F32)
        for b in range(WIN):
            line = jnp.concatenate([t[b : b + 1] for t in evens + odds], 0)
            total = total + pltpu.roll(line, 7 - b, 1)
        both = jnp.concatenate([total, jnp.zeros((8, channels - 128), F32)], 1)
        keep_ref[g, d // 16] = both
        send_ref[g, d // 16] = both

    for g in range(groups):
        group(g)
    for result in results:
        result.wait()


def attention(ncol, flags, packets, weights, halves, table):
    channels, d = weights[1].shape
    own = WIN // 2 * ncol
    piece = jax.ShapeDtypeStruct((2, d // 16 + 1, 8, channels), F32)
    term = jax.ShapeDtypeStruct((2 * own, d), BF16)
    vmem = pl.BlockSpec(memory_space=pltpu.VMEM)
    hbm = pl.BlockSpec(memory_space=pltpu.HBM)
    return pl.pallas_call(
        attention_kernel,
        out_shape=(term, term, piece, piece),
        in_specs=[pl.BlockSpec(memory_space=pltpu.SMEM)] + [hbm] * 6 + [vmem],
        out_specs=(hbm, hbm, vmem, vmem),
        scratch_shapes=[
            pltpu.VMEM((2,) + packets[0].shape, BF16),
            pltpu.VMEM((2, 3, d, channels), BF16),
            pltpu.VMEM((2, channels, d), BF16),
            pltpu.VMEM((2, 2 * own, d), F32),
            pltpu.VMEM((2, 2 * own, d), BF16),
            pltpu.VMEM((WIN, ncol + WIN, channels), F32),
            pltpu.VMEM((WIN, ncol + WIN, channels), F32),
            pltpu.VMEM((WIN * SHIFT, channels), F32),
            pltpu.VMEM((16, channels), BF16),
            pltpu.SemaphoreType.DMA((2 * (3 + d // channels) + 9,)),
        ],
        compiler_params=pltpu.CompilerParams(vmem_limit_bytes=VMEM_LIMIT),
        cost_estimate=pl.CostEstimate(
            flops=3_000_000_000, bytes_accessed=11_000_000, transcendentals=131072
        ),
        name="window_attention",
    )(flags, *packets, *weights, *halves, table)


def pack_kernel(core_ref, wq_ref, wp_ref, tab_ref, out_ref):
    tall, d = wp_ref.shape
    _, half, channels = wq_ref.shape
    for t in range(3):
        out_ref[t * half : (t + 1) * half] = wq_ref[t]
    for j in range(d // channels):
        at = 3 * half + j * tall
        out_ref[at : at + tall] = wp_ref[:, j * channels : (j + 1) * channels]
    table = table_to_rows(tab_ref[...])
    top = table.astype(BF16)
    table = table - top.astype(F32)
    middle = table.astype(BF16)
    table = table - middle.astype(F32)
    low = jnp.concatenate([table, jnp.zeros_like(table)], 1)
    high = jnp.concatenate([top.astype(F32), middle.astype(F32)], 1)
    at = out_ref.shape[0] - 2 * table.shape[0]
    out_ref[at:, : high.shape[1]] = jnp.concatenate([high, low], 0).astype(BF16)


def packed_half(core, w_qkv, w_proj, table):
    _, d, channels = w_qkv.shape
    rows = 3 * d // 2 + d // channels * (channels // 2) + 4 * table.shape[0]
    return pl.pallas_call(
        pack_kernel,
        out_shape=jax.ShapeDtypeStruct((rows, channels), BF16),
        grid_spec=pltpu.PrefetchScalarGridSpec(
            num_scalar_prefetch=1,
            grid=(1,),
            in_specs=[
                pl.BlockSpec((3, d // 2, channels), lambda i, core: (0, core[0], 0)),
                pl.BlockSpec((channels // 2, d), lambda i, core: (core[0], 0)),
                pl.BlockSpec(table.shape, lambda i, core: (0, 0)),
            ],
            out_specs=pl.BlockSpec((rows, channels), lambda i, core: (0, 0)),
        ),
        compiler_params=pltpu.CompilerParams(vmem_limit_bytes=VMEM_LIMIT),
        cost_estimate=pl.CostEstimate(flops=0, bytes_accessed=2_100_000, transcendentals=0),
        name="packed_half",
    )(core, w_qkv, w_proj, table)


def strips_kernel(tokens_ref, grads_ref, out_ref):
    out_ref[...] = jnp.concatenate([tokens_ref[:, :SHIFT], grads_ref[:, :SHIFT]], 1)


def left_strips(tokens, grads):
    prow, ncol, d = tokens.shape
    spec = pl.BlockSpec((prow, 16, d), lambda i: (0, 0, 0))
    return pl.pallas_call(
        strips_kernel,
        grid=(1,),
        out_shape=jax.ShapeDtypeStruct((prow, 2 * SHIFT, d), BF16),
        in_specs=[spec, spec],
        out_specs=pl.BlockSpec((prow, 2 * SHIFT, d), lambda i: (0, 0, 0)),
        compiler_params=pltpu.CompilerParams(vmem_limit_bytes=VMEM_LIMIT),
        cost_estimate=pl.CostEstimate(flops=0, bytes_accessed=300_000, transcendentals=0),
        name="left_strips",
    )(tokens, grads)


def norm_kernel(tokens_ref, grads_ref, strips_ref, gain_ref, valid_ref, out_ref, cols, strip_rows):
    prow, ncol, d = tokens_ref.shape
    own = prow * ncol
    strip = prow * SHIFT
    cols[:, :ncol] = tokens_ref[...].astype(F32)
    for i in range(prow):
        both = strips_ref[i].astype(F32)
        cols[i, ncol : ncol + SHIFT] = both[:SHIFT]
        strip_rows[i * SHIFT : (i + 1) * SHIFT] = both[SHIFT:]
    x = cols[:, SHIFT : SHIFT + ncol].reshape(own, d)
    x = x - jnp.mean(x, -1, keepdims=True)
    rstd = lax.rsqrt(jnp.mean(x * x, -1, keepdims=True) + EPS)
    out_ref[:own] = (x * rstd * gain_ref[...]).astype(BF16)
    out_ref[own : 2 * own] = grads_ref[...].reshape(own, d)
    out_ref[2 * own : 2 * own + strip] = strip_rows[...].astype(BF16)
    out_ref[2 * own + strip :] = jnp.zeros((valid_ref.shape[0], d), BF16)
    out_ref[2 * own + strip :, :ncol] = valid_ref[...].astype(F32).astype(BF16)


def norm(tokens, grads, strips, gain, valid):
    prow, ncol, d = tokens.shape
    strip = prow * SHIFT
    vmem = pl.BlockSpec(memory_space=pltpu.VMEM)
    return pl.pallas_call(
        norm_kernel,
        out_shape=jax.ShapeDtypeStruct((2 * prow * ncol + strip + valid.shape[0], d), BF16),
        in_specs=[vmem] * 5,
        out_specs=vmem,
        scratch_shapes=[pltpu.VMEM((prow, ncol + WIN, d), F32), pltpu.VMEM((strip, d), F32)],
        compiler_params=pltpu.CompilerParams(vmem_limit_bytes=VMEM_LIMIT),
        cost_estimate=pl.CostEstimate(
            flops=1_500_000, bytes_accessed=600_000, transcendentals=128
        ),
        name="layer_norm",
    )(tokens, grads, strips, gain, valid)


def on_device(tokens, valid, gain, w_qkv, w_proj, rel_table, cotangent):
    part_rows, ncol, d = tokens.shape
    n_head = lax.axis_size("head")
    n_row = lax.axis_size("row")
    n_col = lax.axis_size("col")
    tile_rows = part_rows * n_head
    own = part_rows * ncol
    strip = part_rows * SHIFT
    channels = w_proj.shape[0]
    row = lax.axis_index("row")
    col = lax.axis_index("col")
    head = lax.axis_index("head")

    left = [(c, (c - 1) % n_col) for c in range(n_col)]
    right = [(c, (c + 1) % n_col) for c in range(n_col)]
    swap = [(c, c ^ 1) for c in range(n_col)]
    mates = []
    for r in range(n_row):
        low, high = r * n_head, (r + 1) % n_row * n_head
        mates += [(low + 1, low + 2), (low + 2, low + 1), (low + 3, high), (high, low + 3)]
    beside = [(h, h ^ 1) for h in range(n_head)]

    def trade(value):
        return lax.ppermute(value, ("row", "head"), mates)

    last = ((head == 3) & (row == n_row - 1)) | ((head == 0) & (row == 0))
    inner = (head == 1) | (head == 2)
    flags = [last, col == n_col - 1, col % 2 == 1, head % 2 == 0, jnp.logical_not(inner)]
    flags = jnp.stack([flag.astype(jnp.int32) for flag in flags])
    table = rel_table.T
    w_qkv = w_qkv.transpose(1, 0, 2)

    strips = left_strips(tokens, cotangent)
    w_in, _ = lax.optimization_barrier((w_qkv, strips))
    half = lax.ppermute(packed_half((col % 2)[None], w_in, w_proj, table), "head", beside)
    strips = lax.ppermute(strips, "col", left)
    packet = norm(tokens, cotangent, strips, gain[None], valid)
    packets = (packet, trade(packet))
    half, _ = lax.optimization_barrier((half, packets[1]))
    other_half = lax.ppermute(half, "col", swap)

    own_term, mate_term, keep, send = attention(
        ncol, flags, packets, (w_qkv, w_proj), (half, other_half), table
    )
    pairs = keep + lax.ppermute(send, "col", swap)
    mate_term = trade(mate_term)
    pair_beside = lax.ppermute(pairs[1].astype(BF16), "head", beside)
    pair = pairs[0] + pair_beside.astype(F32)

    table_part = jnp.broadcast_to(pair[-1:, :, :128], (d // 16, 8, 128))
    pieces = jnp.concatenate([pair[:-1], table_part], 2).astype(BF16)
    cores = [
        [r * n_col + c for r in range(n_row) for c in range(n_col) if c % 2 == parity]
        for parity in range(2)
    ]
    mate_term, _ = lax.optimization_barrier((mate_term, pieces))
    pieces = lax.all_to_all(pieces, ("row", "col"), 0, 0, axis_index_groups=cores, tiled=True)
    pieces = jnp.sum(pieces.astype(F32), 0)
    scale = 1.0 / math.sqrt(tile_rows * ncol * n_row * n_col)
    proj_grad = pieces[:, :channels].T * scale
    table_grad = rows_to_table(pieces[:, channels:]) * (WIN * scale)

    total = own_term.astype(F32) + mate_term.astype(F32)
    total = total.reshape(2, part_rows, ncol, d)
    edges = lax.ppermute(total[:, :, -SHIFT:].astype(BF16), "col", right).astype(F32)
    total = jnp.concatenate([edges, total[:, :, :-SHIFT]], 2)
    norm_grad = total[0]

    flat = tokens.astype(F32)
    mean = jnp.mean(flat, -1, keepdims=True)
    centered = flat - mean
    rstd = lax.rsqrt(jnp.mean(centered * centered, -1, keepdims=True) + EPS)
    xhat = centered * rstd
    scaled = norm_grad * gain
    token_gradient = cotangent.astype(F32) + rstd * (
        scaled
        - jnp.mean(scaled, -1, keepdims=True)
        - xhat * jnp.mean(scaled * xhat, -1, keepdims=True)
    )

    mixed = (flat + total[1]).astype(BF16)
    return (mixed, token_gradient.astype(BF16), proj_grad, table_grad)


def solution(mesh):
    return jax.shard_map(
        on_device,
        mesh=mesh,
        in_specs=(
            P(("row", "head"), "col", None),
            P("row", "col"),
            P(),
            P(None, None, "head"),
            P("head", None),
            P(None, "head"),
            P(("row", "head"), "col", None),
        ),
        out_specs=(
            P(("row", "head"), "col", None),
            P(("row", "head"), "col", None),
            P("head", ("row", "col")),
            P(None, "head"),
        ),
        check_vma=False,
    )
```

```python
import math

import jax
import jax.numpy as jnp
from jax import lax
from jax.experimental import pallas as pl
from jax.experimental.pallas import tpu as pltpu
from jax.sharding import PartitionSpec as P

HD = 64
WIN = 8
SHIFT = 4
EPS = 1e-05
F32 = jnp.float32
BF16 = jnp.bfloat16
SPAN = 2 * WIN - 1
POS = WIN * WIN
VMEM_LIMIT = 56 * 1024 * 1024


def dot(a, b, ca, cb):
    return lax.dot_general(a, b, (((ca,), (cb,)), ((), ())), preferred_element_type=F32)


def rows_to_table(vectors):
    heads = vectors.shape[0] // 2
    even = vectors[:heads].reshape(heads, 8, 16)
    odd = jnp.concatenate([vectors[heads:, 8:], vectors[heads:, :8]], 1).reshape(heads, 8, 16)
    both = jnp.stack([even, odd], 2).reshape(heads, 16, 16)[:, :SPAN, :SPAN]
    return both.reshape(heads, SPAN * SPAN).T


def table_to_rows(table):
    heads, count = table.shape
    table = jnp.concatenate([table, jnp.zeros((heads, 256 - count), F32)], 1)
    table = jnp.concatenate([table, table], 0)
    lane = lax.broadcasted_iota(jnp.int32, (2 * heads, 128), 1)
    odd = lax.broadcasted_iota(jnp.int32, (2 * heads, 128), 0) >= heads
    rows = jnp.zeros((2 * heads, 128), F32)
    for a in range(SPAN):
        moved = pltpu.roll(table, (-a * (SPAN - 8)) % 256, 1)[:, :128]
        here = (lane >= 8 * a) & (lane < 8 * a + SPAN) & (odd == (a % 2 == 1))
        rows = jnp.where(here, moved, rows)
    return rows


def attention_kernel(
    flags_ref, t_own, t_other, c_own, c_other, s_own, s_other, wq_in, wp_in,
    half_in, other_half_in, tab_ref, gain_ref, valid_ref, valid_other_ref,
    own_out, other_out, keep_out, send_out,
    keep_ref, send_ref, ts_ref, cs_ref, strips_ref, xn_ref, cols, strip_rows, wq_all, wp_all, sum_ref, out_ref, grad_cols, attn_cols, attn_edge, tab_parts, sems,
):
    groups, channels, d = wp_all.shape
    heads = channels // HD
    scale = HD ** (-0.5)
    parts, own = cs_ref.shape[:2]
    ncol = grad_cols.shape[1] - WIN
    prow = own // ncol
    wins = ncol // WIN
    rows = own * parts
    lanes = heads * POS
    last_row = flags_ref[0] == 1
    last_col = flags_ref[1] == 1
    core = flags_ref[2]
    own_slot = flags_ref[3]
    band = flags_ref[4]

    half = d // 2
    tall = channels // 2
    moves = [
        (s_own, strips_ref.at[own_slot]),
        (s_other, strips_ref.at[1 - own_slot]),
        (t_own, ts_ref.at[own_slot]),
        (t_other, ts_ref.at[1 - own_slot]),
        (wp_in, wp_all.at[0]),
        (c_own, cs_ref.at[own_slot]),
        (c_other, cs_ref.at[1 - own_slot]),
        (wq_in, wq_all.at[0]),
    ]
    first_moves = len(moves)
    for source, at in ((half_in, core), (other_half_in, 1 - core)):
        rows_at = pl.ds(pl.multiple_of(at * half, half), half)
        for t in range(3):
            piece = source.at[t * half : (t + 1) * half, :]
            moves.append((piece, wq_all.at[1, t, rows_at, :]))
        rows_at = pl.ds(pl.multiple_of(at * tall, tall), tall)
        for j in range(d // channels):
            piece = source.at[3 * half + j * tall : 3 * half + (j + 1) * tall, :]
            span = slice(j * channels, (j + 1) * channels)
            moves.append((piece, wp_all.at[1, rows_at, span]))
    moves.append((half_in.at[half_in.shape[0] - 16 :, :], tab_parts))
    moves = [pltpu.make_async_copy(a, b, sems.at[i]) for i, (a, b) in enumerate(moves)]
    for move in moves:
        move.start()

    lane128 = lax.broadcasted_iota(jnp.int32, (8, 128), 1)
    even_lane = ((lane128 // 8) % 2) == 0

    def bias_of(tab):
        shifted = [pltpu.roll(tab, (b - 7) % 128, 1) for b in range(WIN)]
        per_head = []
        for h in range(heads):
            ev = jnp.concatenate([s[h : h + 1] for s in shifted], 0)
            od = jnp.concatenate([s[heads + h : heads + h + 1] for s in shifted], 0)
            per_head.append(jnp.where(even_lane, ev, od))
        bias_rows = []
        for a in range(WIN):
            pieces = []
            for p in range(heads // 2):
                lo = pltpu.roll(per_head[2 * p], (-(7 - a) * 8) % 128, 1)
                hi = pltpu.roll(per_head[2 * p + 1], (64 - (7 - a) * 8) % 128, 1)
                pieces.append(jnp.where(lane128 < 64, lo, hi))
            bias_rows.append(jnp.concatenate(pieces, 1))
        return jnp.concatenate(bias_rows, 0)

    key_pos = lax.broadcasted_iota(jnp.int32, (POS, lanes), 0)
    query_pos = lax.broadcasted_iota(jnp.int32, (POS, lanes), 1) % POS
    same_pos = key_pos == query_pos
    same_row_half = (key_pos // (WIN * SHIFT)) == (query_pos // (WIN * SHIFT))
    same_col_half = ((key_pos // SHIFT) % 2) == ((query_pos // SHIFT) % 2)
    lane_head = lax.broadcasted_iota(jnp.int32, (POS, channels), 1) // HD
    head_f = [(lane_head == h).astype(F32) for h in range(heads)]
    head_b = [m.astype(BF16) for m in head_f]

    results = [
        pltpu.make_async_copy(out_ref.at[own_slot], own_out, sems.at[len(moves)]),
        pltpu.make_async_copy(out_ref.at[1 - own_slot], other_out, sems.at[len(moves) + 1]),
    ]
    for g in range(groups):
        for j, (source, target) in enumerate(((keep_ref, keep_out), (send_ref, send_out))):
            sem = sems.at[len(moves) + 2 + 2 * g + j]
            results.append(pltpu.make_async_copy(source.at[g], target.at[g], sem))

    def group(g):
        if g == 0:
            bias = bias_of(table_to_rows(tab_ref[...]))
        for move in moves[:4] if g == 0 else moves[first_moves:]:
            move.wait()
        if g == 1:
            terms = tab_parts[...].astype(F32)
            bias = bias_of(terms[:8, :128] + terms[:8, 128:256] + terms[8:, :128])
        if g == 0:
            for x in range(parts):
                block = ts_ref[x].astype(F32).reshape(prow, ncol, d)
                cols[x * prow : (x + 1) * prow, :ncol] = block
                for i in range(prow):
                    both = strips_ref[x, i].astype(F32)
                    at = x * prow + i
                    cols[at, ncol : ncol + SHIFT] = both[:SHIFT]
                    strip_rows[at * SHIFT : (at + 1) * SHIFT] = both[SHIFT:]
            moved = cols[:, SHIFT : SHIFT + ncol].reshape(rows, d)
            moved = moved - jnp.mean(moved, -1, keepdims=True)
            rstd = lax.rsqrt(jnp.mean(moved * moved, -1, keepdims=True) + EPS)
            xn_ref[...] = (moved * rstd * gain_ref[...]).astype(BF16)
            for move in moves[4:first_moves]:
                move.wait()

        edge = strip_rows[...].astype(BF16)
        wp = wp_all[g]
        edge_grad = dot(edge, wp, 1, 1)
        attn_edge[...] = edge_grad

        ds_total = jnp.zeros((POS, lanes), F32)
        xn = xn_ref[...]
        ct = cs_ref[...].reshape(rows, d)
        queries, keys, values = [
            dot(xn, wq_all[g, t], 1, 0).reshape(WIN, wins, WIN, channels) for t in range(3)
        ]
        marks = jnp.where(flags_ref[5] == 1, valid_other_ref[...], valid_ref[...])
        key_row = lax.broadcasted_iota(jnp.int32, (POS, marks.shape[0]), 0) // WIN + band * WIN
        tile_row = lax.broadcasted_iota(jnp.int32, (POS, marks.shape[0]), 1)
        marks = dot((key_row == tile_row).astype(BF16), marks.astype(BF16), 1, 0)
        key_col = lax.broadcasted_iota(jnp.int32, marks.shape, 0) % WIN
        tile_col = lax.broadcasted_iota(jnp.int32, marks.shape, 1)
        grad_cols[:, :ncol] = dot(ct, wp, 1, 1).reshape(WIN, ncol, channels)
        for i in range(WIN):
            grad_cols[i, ncol : ncol + SHIFT] = attn_edge[i * SHIFT : (i + 1) * SHIFT]
        dog = grad_cols[:, SHIFT : SHIFT + ncol].reshape(WIN, wins, WIN, channels)
        outs, dqs, dks, dvs = [], [], [], []
        for u in range(wins):
            q = queries[:, u].reshape(POS, channels).astype(BF16)
            k = keys[:, u].reshape(POS, channels).astype(BF16)
            v = values[:, u].reshape(POS, channels).astype(BF16)
            do = dog[:, u].reshape(POS, channels).astype(BF16)
            qbd = jnp.concatenate([q * m for m in head_b], 0)
            dbd = jnp.concatenate([do * m for m in head_b], 0)
            s = dot(k, qbd, 1, 1) * scale + bias
            valid = jnp.where(tile_col == key_col + u * WIN, marks, 0.0)
            valid = jnp.sum(valid, 1, keepdims=True)
            allowed = same_pos | (jnp.broadcast_to(valid, (POS, lanes)) == 1.0)
            allowed = allowed & (same_row_half | jnp.logical_not(last_row))
            if u == wins - 1:
                allowed = allowed & (same_col_half | jnp.logical_not(last_col))
            s = jnp.where(allowed, s, -1e30)
            e = jnp.exp(s - jnp.max(s, 0, keepdims=True))
            p = e / jnp.sum(e, 0, keepdims=True)
            pb = p.astype(BF16)
            dp = dot(v, dbd, 1, 1)
            ds = p * (dp - jnp.sum(p * dp, 0, keepdims=True))
            dsb = ds.astype(BF16)
            ds_total = ds_total + ds
            dvs.append(dot(pb, dbd, 1, 0))
            dks.append(dot(dsb, qbd, 1, 0) * scale)
            o_all = dot(pb, v, 0, 0)
            dq_all = dot(dsb, k, 0, 0)
            o = o_all[:POS] * head_f[0]
            dq = dq_all[:POS] * head_f[0]
            for h in range(1, heads):
                o = o + o_all[h * POS : (h + 1) * POS] * head_f[h]
                dq = dq + dq_all[h * POS : (h + 1) * POS] * head_f[h]
            outs.append(o)
            dqs.append(dq * scale)

        def patches(pieces):
            pieces = [z.reshape(WIN, 1, WIN, channels) for z in pieces]
            return jnp.concatenate(pieces, 1).reshape(rows, channels)

        attn = patches(outs)
        back = dot(patches(dqs).astype(BF16), wq_all[g, 0], 1, 1)
        back = back + dot(patches(dks).astype(BF16), wq_all[g, 1], 1, 1)
        back = back + dot(patches(dvs).astype(BF16), wq_all[g, 2], 1, 1)
        branch = dot(attn.astype(BF16), wp, 1, 0)
        for j, term in enumerate((back, branch)):
            term = term.reshape(parts, own, d)
            at = slice(j * own, (j + 1) * own)
            if g < groups - 1:
                sum_ref[:, at] = term
            else:
                out_ref[:, at] = (sum_ref[:, at] + term).astype(BF16)
        if g == groups - 1:
            for result in results[:2]:
                result.start()
        attn_cols[:, :SHIFT] = jnp.zeros((WIN, SHIFT, channels), F32)
        attn_cols[:, SHIFT : SHIFT + ncol] = attn.reshape(WIN, ncol, channels)
        for i in range(WIN):
            attn_edge[i * SHIFT : (i + 1) * SHIFT] = attn_cols[i, ncol : ncol + SHIFT]
        wt = dot(ct, attn_cols[:, :ncol].reshape(rows, channels).astype(BF16), 0, 0)
        wt = wt + dot(edge, attn_edge[...].astype(BF16), 0, 0)
        halves = wt.reshape(d // 16, 2, 8, channels)
        first = core == 0
        low, high = halves[:, 0].astype(BF16), halves[:, 1].astype(BF16)
        keep_ref[g, : d // 16] = jnp.where(first, low, high)
        send_ref[g, : d // 16] = jnp.where(first, high, low)

        diag = [jnp.zeros((8, 128), F32) for _ in range(heads)]
        for a in range(WIN):
            for p in range(heads // 2):
                block = ds_total[8 * a : 8 * a + 8, 128 * p : 128 * p + 128]
                lo = jnp.where(lane128 < 64, block, 0.0)
                hi = jnp.where(lane128 < 64, 0.0, block)
                diag[2 * p] = diag[2 * p] + pltpu.roll(lo, (7 - a) * 8, 1)
                diag[2 * p + 1] = diag[2 * p + 1] + pltpu.roll(hi, ((7 - a) * 8 - 64) % 128, 1)
        evens = [jnp.where(even_lane, t, 0.0) for t in diag]
        odds = [jnp.where(even_lane, 0.0, t) for t in diag]
        total = jnp.zeros((8, 128), F32)
        for b in range(WIN):
            line = jnp.concatenate([t[b : b + 1] for t in evens + odds], 0)
            total = total + pltpu.roll(line, 7 - b, 1)
        both = jnp.concatenate([total, jnp.zeros((8, channels - 128), F32)], 1)
        both = both.astype(BF16)
        keep_ref[g, d // 16] = both
        send_ref[g, d // 16] = both
        for result in results[2 + 2 * g : 4 + 2 * g]:
            result.start()

    for g in range(groups):
        group(g)
    for result in results:
        result.wait()


def attention(flags, tokens, grads, strips, weights, halves, table, gain, valids):
    channels, d = weights[1].shape
    own = grads[0].shape[0]
    ncol = own // strips[0].shape[0]
    piece = jax.ShapeDtypeStruct((2, d // 16 + 1, 8, channels), BF16)
    term = jax.ShapeDtypeStruct((2 * own, d), BF16)
    vmem = pl.BlockSpec(memory_space=pltpu.VMEM)
    hbm = pl.BlockSpec(memory_space=pltpu.HBM)
    return pl.pallas_call(
        attention_kernel,
        out_shape=(term, term, piece, piece),
        in_specs=[pl.BlockSpec(memory_space=pltpu.SMEM)] + [hbm] * 10 + [vmem] * 4,
        out_specs=(hbm,) * 4,
        scratch_shapes=[
            pltpu.VMEM(piece.shape, BF16),
            pltpu.VMEM(piece.shape, BF16),
            pltpu.VMEM((2, own, d), BF16),
            pltpu.VMEM((2, own, d), BF16),
            pltpu.VMEM((2,) + strips[0].shape, BF16),
            pltpu.VMEM((2 * own, d), BF16),
            pltpu.VMEM((WIN, ncol + WIN, d), F32),
            pltpu.VMEM((WIN * SHIFT, d), F32),
            pltpu.VMEM((2, 3, d, channels), BF16),
            pltpu.VMEM((2, channels, d), BF16),
            pltpu.VMEM((2, 2 * own, d), F32),
            pltpu.VMEM((2, 2 * own, d), BF16),
            pltpu.VMEM((WIN, ncol + WIN, channels), F32),
            pltpu.VMEM((WIN, ncol + WIN, channels), F32),
            pltpu.VMEM((WIN * SHIFT, channels), F32),
            pltpu.VMEM((16, channels), BF16),
            pltpu.SemaphoreType.DMA((2 * (3 + d // channels) + 15,)),
        ],
        compiler_params=pltpu.CompilerParams(vmem_limit_bytes=VMEM_LIMIT),
        cost_estimate=pl.CostEstimate(
            flops=3_000_000_000, bytes_accessed=11_000_000, transcendentals=131072
        ),
        name="window_attention",
    )(flags, *tokens, *grads, *strips, *weights, *halves, table, gain, *valids)


def pack_kernel(core_ref, wq_ref, wp_ref, tab_ref, out_ref):
    tall, d = wp_ref.shape
    _, half, channels = wq_ref.shape
    for t in range(3):
        out_ref[t * half : (t + 1) * half] = wq_ref[t]
    for j in range(d // channels):
        at = 3 * half + j * tall
        out_ref[at : at + tall] = wp_ref[:, j * channels : (j + 1) * channels]
    table = table_to_rows(tab_ref[...])
    top = table.astype(BF16)
    table = table - top.astype(F32)
    middle = table.astype(BF16)
    table = table - middle.astype(F32)
    low = jnp.concatenate([table, jnp.zeros_like(table)], 1)
    high = jnp.concatenate([top.astype(F32), middle.astype(F32)], 1)
    at = out_ref.shape[0] - 2 * table.shape[0]
    out_ref[at:, : high.shape[1]] = jnp.concatenate([high, low], 0).astype(BF16)


def packed_half(core, w_qkv, w_proj, table):
    _, d, channels = w_qkv.shape
    rows = 3 * d // 2 + d // channels * (channels // 2) + 4 * table.shape[0]
    return pl.pallas_call(
        pack_kernel,
        out_shape=jax.ShapeDtypeStruct((rows, channels), BF16),
        grid_spec=pltpu.PrefetchScalarGridSpec(
            num_scalar_prefetch=1,
            grid=(1,),
            in_specs=[
                pl.BlockSpec((3, d // 2, channels), lambda i, core: (0, core[0], 0)),
                pl.BlockSpec((channels // 2, d), lambda i, core: (core[0], 0)),
                pl.BlockSpec(table.shape, lambda i, core: (0, 0)),
            ],
            out_specs=pl.BlockSpec((rows, channels), lambda i, core: (0, 0)),
        ),
        compiler_params=pltpu.CompilerParams(vmem_limit_bytes=VMEM_LIMIT),
        cost_estimate=pl.CostEstimate(flops=0, bytes_accessed=2_100_000, transcendentals=0),
        name="packed_half",
    )(core, w_qkv, w_proj, table)


def strips_kernel(tokens_ref, grads_ref, out_ref):
    out_ref[...] = jnp.concatenate([tokens_ref[:, :SHIFT], grads_ref[:, :SHIFT]], 1)


def left_strips(tokens, grads):
    prow, ncol, d = tokens.shape
    spec = pl.BlockSpec((prow, 16, d), lambda i: (0, 0, 0))
    return pl.pallas_call(
        strips_kernel,
        grid=(1,),
        out_shape=jax.ShapeDtypeStruct((prow, 2 * SHIFT, d), BF16),
        in_specs=[spec, spec],
        out_specs=pl.BlockSpec((prow, 2 * SHIFT, d), lambda i: (0, 0, 0)),
        compiler_params=pltpu.CompilerParams(vmem_limit_bytes=VMEM_LIMIT),
        cost_estimate=pl.CostEstimate(flops=0, bytes_accessed=300_000, transcendentals=0),
        name="left_strips",
    )(tokens, grads)


def on_device(tokens, valid, gain, w_qkv, w_proj, rel_table, cotangent):
    part_rows, ncol, d = tokens.shape
    n_head = lax.axis_size("head")
    n_row = lax.axis_size("row")
    n_col = lax.axis_size("col")
    tile_rows = part_rows * n_head
    own = part_rows * ncol
    strip = part_rows * SHIFT
    channels = w_proj.shape[0]
    row = lax.axis_index("row")
    col = lax.axis_index("col")
    head = lax.axis_index("head")

    right = [(c, (c + 1) % n_col) for c in range(n_col)]
    swap = [(c, c ^ 1) for c in range(n_col)]
    mates = []
    for r in range(n_row):
        low, high = r * n_head, (r + 1) % n_row * n_head
        mates += [(low + 1, low + 2), (low + 2, low + 1), (low + 3, high), (high, low + 3)]
    beside = [(h, h ^ 1) for h in range(n_head)]

    def trade(value):
        return lax.ppermute(value, ("row", "head"), mates)

    last = ((head == 3) & (row == n_row - 1)) | ((head == 0) & (row == 0))
    inner = (head == 1) | (head == 2)
    flags = [last, col == n_col - 1, col % 2 == 1, head % 2 == 0, jnp.logical_not(inner), head == 0]
    flags = jnp.stack([flag.astype(jnp.int32) for flag in flags])
    table = rel_table.T
    w_qkv = w_qkv.transpose(1, 0, 2)

    half = lax.ppermute(packed_half((col % 2)[None], w_qkv, w_proj, table), "head", beside)
    strips = left_strips(tokens, cotangent)
    whole = ("row", "col", "head")
    holder = {a: b for a, b in mates}

    def place(line_head, c):
        return (line_head // n_head * n_col + c) * n_head + line_head % n_head

    spots = [(i, c) for i in range(n_row * n_head) for c in range(n_col)]
    straight = [(place(i, (c + 1) % n_col), place(i, c)) for i, c in spots]
    across = [(place(holder[i], (c + 1) % n_col), place(i, c)) for i, c in spots]
    strips = (lax.ppermute(strips, whole, straight), lax.ppermute(strips, whole, across))
    grads = cotangent.reshape(own, d)
    grads = (grads, trade(grads))
    patches = tokens.reshape(own, d)
    patches = (patches, trade(patches))
    marks = valid.astype(F32)
    down = [(r * n_head, (r + 1) % n_row * n_head) for r in range(n_row)]
    marks = (marks, lax.ppermute(marks, ("row", "head"), down))
    half, *_ = lax.optimization_barrier((half, patches[1], grads[1], *strips, marks[1]))
    other_half = lax.ppermute(half, "col", swap)

    own_term, mate_term, keep, send = attention(
        flags,
        patches,
        grads,
        strips,
        (w_qkv, w_proj),
        (half, other_half),
        table,
        gain[None],
        marks,
    )
    pairs = keep.astype(F32) + lax.ppermute(send, "col", swap).astype(F32)
    mate_term = trade(mate_term)
    pair_beside = lax.ppermute(pairs[1].astype(BF16), "head", beside)
    pair = pairs[0] + pair_beside.astype(F32)

    table_part = jnp.broadcast_to(pair[-1:, :, :128], (d // 16, 8, 128))
    pieces = jnp.concatenate([pair[:-1], table_part], 2).astype(BF16)
    cores = [
        [r * n_col + c for r in range(n_row) for c in range(n_col) if c % 2 == parity]
        for parity in range(2)
    ]
    mate_term, _ = lax.optimization_barrier((mate_term, pieces))
    pieces = lax.all_to_all(pieces, ("row", "col"), 0, 0, axis_index_groups=cores, tiled=True)
    pieces = jnp.sum(pieces.astype(F32), 0)
    scale = 1.0 / math.sqrt(tile_rows * ncol * n_row * n_col)
    proj_grad = pieces[:, :channels].T * scale
    table_grad = rows_to_table(pieces[:, channels:]) * (WIN * scale)

    total = own_term.astype(F32) + mate_term.astype(F32)
    total = total.reshape(2, part_rows, ncol, d)
    edges = lax.ppermute(total[:, :, -SHIFT:].astype(BF16), "col", right).astype(F32)
    total = jnp.concatenate([edges, total[:, :, :-SHIFT]], 2)
    norm_grad = total[0]

    flat = tokens.astype(F32)
    mean = jnp.mean(flat, -1, keepdims=True)
    centered = flat - mean
    rstd = lax.rsqrt(jnp.mean(centered * centered, -1, keepdims=True) + EPS)
    xhat = centered * rstd
    scaled = norm_grad * gain
    token_gradient = cotangent.astype(F32) + rstd * (
        scaled
        - jnp.mean(scaled, -1, keepdims=True)
        - xhat * jnp.mean(scaled * xhat, -1, keepdims=True)
    )

    mixed = (flat + total[1]).astype(BF16)
    return (mixed, token_gradient.astype(BF16), proj_grad, table_grad)


def solution(mesh):
    return jax.shard_map(
        on_device,
        mesh=mesh,
        in_specs=(
            P(("row", "head"), "col", None),
            P("row", "col"),
            P(),
            P(None, None, "head"),
            P("head", None),
            P(None, "head"),
            P(("row", "head"), "col", None),
        ),
        out_specs=(
            P(("row", "head"), "col", None),
            P(("row", "head"), "col", None),
            P("head", ("row", "col")),
            P(None, "head"),
        ),
        check_vma=False,
    )
```

```python
import math

import jax
import jax.numpy as jnp
from jax import lax
from jax.experimental import pallas as pl
from jax.experimental.pallas import tpu as pltpu
from jax.sharding import PartitionSpec as P

HD = 64
WIN = 8
SHIFT = 4
EPS = 1e-05
F32 = jnp.float32
BF16 = jnp.bfloat16
SPAN = 2 * WIN - 1
POS = WIN * WIN
VMEM_LIMIT = 56 * 1024 * 1024
STRIPS_VMEM_LIMIT = 4 * 1024 * 1024
MAIN_VMEM_LIMIT = 36 * 1024 * 1024


def dot(a, b, ca, cb):
    return lax.dot_general(a, b, (((ca,), (cb,)), ((), ())), preferred_element_type=F32)


def rows_to_table(vectors):
    heads = vectors.shape[0] // 2
    even = vectors[:heads].reshape(heads, 8, 16)
    odd = jnp.concatenate([vectors[heads:, 8:], vectors[heads:, :8]], 1).reshape(heads, 8, 16)
    both = jnp.stack([even, odd], 2).reshape(heads, 16, 16)[:, :SPAN, :SPAN]
    return both.reshape(heads, SPAN * SPAN).T


def table_to_rows(table):
    heads, count = table.shape
    table = jnp.concatenate([table, jnp.zeros((heads, 256 - count), F32)], 1)
    table = jnp.concatenate([table, table], 0)
    lane = lax.broadcasted_iota(jnp.int32, (2 * heads, 128), 1)
    odd = lax.broadcasted_iota(jnp.int32, (2 * heads, 128), 0) >= heads
    rows = jnp.zeros((2 * heads, 128), F32)
    for a in range(SPAN):
        moved = pltpu.roll(table, (-a * (SPAN - 8)) % 256, 1)[:, :128]
        here = (lane >= 8 * a) & (lane < 8 * a + SPAN) & (odd == (a % 2 == 1))
        rows = jnp.where(here, moved, rows)
    return rows


def attention_kernel(
    flags_ref, t_own, t_other, c_own, c_other, s_own, s_other, wq_in, wp_in,
    half_in, other_half_in, tab_ref, gain_ref, valid_ref, valid_other_ref,
    own_out, other_out, keep_out, send_out,
    keep_ref, send_ref, ts_ref, cs_ref, strips_ref, xn_ref, cols, strip_rows, wq_all, wp_all, sum_ref, out_ref, grad_cols, attn_cols, attn_edge, tab_parts, sems,
):
    groups, channels, d = wp_all.shape
    heads = channels // HD
    scale = HD ** (-0.5)
    parts, own = cs_ref.shape[:2]
    ncol = grad_cols.shape[1] - WIN
    prow = own // ncol
    wins = ncol // WIN
    rows = own * parts
    lanes = heads * POS
    last_row = flags_ref[0] == 1
    last_col = flags_ref[1] == 1
    core = flags_ref[2]
    own_slot = flags_ref[3]
    band = flags_ref[4]

    half = d // 2
    tall = channels // 2
    moves = [
        (s_own, strips_ref.at[own_slot]),
        (s_other, strips_ref.at[1 - own_slot]),
        (t_own, ts_ref.at[own_slot]),
        (t_other, ts_ref.at[1 - own_slot]),
        (wp_in, wp_all.at[0]),
        (c_own, cs_ref.at[own_slot]),
        (c_other, cs_ref.at[1 - own_slot]),
        (wq_in, wq_all.at[0]),
    ]
    first_moves = len(moves)
    for source, at in ((half_in, core), (other_half_in, 1 - core)):
        rows_at = pl.ds(pl.multiple_of(at * half, half), half)
        for t in range(3):
            piece = source.at[t * half : (t + 1) * half, :]
            moves.append((piece, wq_all.at[1, t, rows_at, :]))
        rows_at = pl.ds(pl.multiple_of(at * tall, tall), tall)
        for j in range(d // channels):
            piece = source.at[3 * half + j * tall : 3 * half + (j + 1) * tall, :]
            span = slice(j * channels, (j + 1) * channels)
            moves.append((piece, wp_all.at[1, rows_at, span]))
    moves.append((half_in.at[half_in.shape[0] - 16 :, :], tab_parts))
    moves = [pltpu.make_async_copy(a, b, sems.at[i]) for i, (a, b) in enumerate(moves)]
    for move in moves:
        move.start()

    lane128 = lax.broadcasted_iota(jnp.int32, (8, 128), 1)
    even_lane = ((lane128 // 8) % 2) == 0

    def bias_of(tab):
        shifted = [pltpu.roll(tab, (b - 7) % 128, 1) for b in range(WIN)]
        per_head = []
        for h in range(heads):
            ev = jnp.concatenate([s[h : h + 1] for s in shifted], 0)
            od = jnp.concatenate([s[heads + h : heads + h + 1] for s in shifted], 0)
            per_head.append(jnp.where(even_lane, ev, od))
        bias_rows = []
        for a in range(WIN):
            pieces = []
            for p in range(heads // 2):
                lo = pltpu.roll(per_head[2 * p], (-(7 - a) * 8) % 128, 1)
                hi = pltpu.roll(per_head[2 * p + 1], (64 - (7 - a) * 8) % 128, 1)
                pieces.append(jnp.where(lane128 < 64, lo, hi))
            bias_rows.append(jnp.concatenate(pieces, 1))
        return jnp.concatenate(bias_rows, 0)

    key_pos = lax.broadcasted_iota(jnp.int32, (POS, lanes), 0)
    query_pos = lax.broadcasted_iota(jnp.int32, (POS, lanes), 1) % POS
    same_pos = key_pos == query_pos
    same_row_half = (key_pos // (WIN * SHIFT)) == (query_pos // (WIN * SHIFT))
    same_col_half = ((key_pos // SHIFT) % 2) == ((query_pos // SHIFT) % 2)
    lane_head = lax.broadcasted_iota(jnp.int32, (POS, channels), 1) // HD
    head_f = [(lane_head == h).astype(F32) for h in range(heads)]
    head_b = [m.astype(BF16) for m in head_f]

    results = [
        pltpu.make_async_copy(out_ref.at[own_slot], own_out, sems.at[len(moves)]),
        pltpu.make_async_copy(out_ref.at[1 - own_slot], other_out, sems.at[len(moves) + 1]),
    ]
    for g in range(groups):
        for j, (source, target) in enumerate(((keep_ref, keep_out), (send_ref, send_out))):
            sem = sems.at[len(moves) + 2 + 2 * g + j]
            results.append(pltpu.make_async_copy(source.at[g], target.at[g], sem))

    def group(g):
        if g == 0:
            bias = bias_of(table_to_rows(tab_ref[...]))
        for move in moves[:4] if g == 0 else moves[first_moves:]:
            move.wait()
        if g == 1:
            terms = tab_parts[...].astype(F32)
            bias = bias_of(terms[:8, :128] + terms[:8, 128:256] + terms[8:, :128])
        if g == 0:
            for x in range(parts):
                block = ts_ref[x].astype(F32).reshape(prow, ncol, d)
                cols[x * prow : (x + 1) * prow, :ncol] = block
                for i in range(prow):
                    both = strips_ref[x, i].astype(F32)
                    at = x * prow + i
                    cols[at, ncol : ncol + SHIFT] = both[:SHIFT]
                    strip_rows[at * SHIFT : (at + 1) * SHIFT] = both[SHIFT:]
            moved = cols[:, SHIFT : SHIFT + ncol].reshape(rows, d)
            moved = moved - jnp.mean(moved, -1, keepdims=True)
            rstd = lax.rsqrt(jnp.mean(moved * moved, -1, keepdims=True) + EPS)
            xn_ref[...] = (moved * rstd * gain_ref[...]).astype(BF16)
            for move in moves[4:first_moves]:
                move.wait()

        edge = strip_rows[...].astype(BF16)
        wp = wp_all[g]
        edge_grad = dot(edge, wp, 1, 1)
        attn_edge[...] = edge_grad

        ds_total = jnp.zeros((POS, lanes), F32)
        xn = xn_ref[...]
        ct = cs_ref[...].reshape(rows, d)
        queries, keys, values = [
            dot(xn, wq_all[g, t], 1, 0).reshape(WIN, wins, WIN, channels) for t in range(3)
        ]
        marks = jnp.where(flags_ref[5] == 1, valid_other_ref[...], valid_ref[...])
        key_row = lax.broadcasted_iota(jnp.int32, (POS, marks.shape[0]), 0) // WIN + band * WIN
        tile_row = lax.broadcasted_iota(jnp.int32, (POS, marks.shape[0]), 1)
        marks = dot((key_row == tile_row).astype(BF16), marks.astype(BF16), 1, 0)
        key_col = lax.broadcasted_iota(jnp.int32, marks.shape, 0) % WIN
        tile_col = lax.broadcasted_iota(jnp.int32, marks.shape, 1)
        grad_cols[:, :ncol] = dot(ct, wp, 1, 1).reshape(WIN, ncol, channels)
        for i in range(WIN):
            grad_cols[i, ncol : ncol + SHIFT] = attn_edge[i * SHIFT : (i + 1) * SHIFT]
        dog = grad_cols[:, SHIFT : SHIFT + ncol].reshape(WIN, wins, WIN, channels)
        outs, dqs, dks, dvs = [], [], [], []
        for u in range(wins):
            q = queries[:, u].reshape(POS, channels).astype(BF16)
            k = keys[:, u].reshape(POS, channels).astype(BF16)
            v = values[:, u].reshape(POS, channels).astype(BF16)
            do = dog[:, u].reshape(POS, channels).astype(BF16)
            qbd = jnp.concatenate([q * m for m in head_b], 0)
            dbd = jnp.concatenate([do * m for m in head_b], 0)
            s = dot(k, qbd, 1, 1) * scale + bias
            valid = jnp.where(tile_col == key_col + u * WIN, marks, 0.0)
            valid = jnp.sum(valid, 1, keepdims=True)
            allowed = same_pos | (jnp.broadcast_to(valid, (POS, lanes)) == 1.0)
            allowed = allowed & (same_row_half | jnp.logical_not(last_row))
            if u == wins - 1:
                allowed = allowed & (same_col_half | jnp.logical_not(last_col))
            s = jnp.where(allowed, s, -1e30)
            e = jnp.exp(s - jnp.max(s, 0, keepdims=True))
            p = e / jnp.sum(e, 0, keepdims=True)
            pb = p.astype(BF16)
            dp = dot(v, dbd, 1, 1)
            ds = p * (dp - jnp.sum(p * dp, 0, keepdims=True))
            dsb = ds.astype(BF16)
            ds_total = ds_total + ds
            dvs.append(dot(pb, dbd, 1, 0))
            dks.append(dot(dsb, qbd, 1, 0) * scale)
            o_all = dot(pb, v, 0, 0)
            dq_all = dot(dsb, k, 0, 0)
            o = o_all[:POS] * head_f[0]
            dq = dq_all[:POS] * head_f[0]
            for h in range(1, heads):
                o = o + o_all[h * POS : (h + 1) * POS] * head_f[h]
                dq = dq + dq_all[h * POS : (h + 1) * POS] * head_f[h]
            outs.append(o)
            dqs.append(dq * scale)

        def patches(pieces):
            pieces = [z.reshape(WIN, 1, WIN, channels) for z in pieces]
            return jnp.concatenate(pieces, 1).reshape(rows, channels)

        attn = patches(outs)
        back = dot(patches(dqs).astype(BF16), wq_all[g, 0], 1, 1)
        back = back + dot(patches(dks).astype(BF16), wq_all[g, 1], 1, 1)
        back = back + dot(patches(dvs).astype(BF16), wq_all[g, 2], 1, 1)
        branch = dot(attn.astype(BF16), wp, 1, 0)
        for j, term in enumerate((back, branch)):
            term = term.reshape(parts, own, d)
            at = slice(j * own, (j + 1) * own)
            if g < groups - 1:
                sum_ref[:, at] = term
            else:
                out_ref[:, at] = (sum_ref[:, at] + term).astype(BF16)
        if g == groups - 1:
            for result in results[:2]:
                result.start()
        attn_cols[:, :SHIFT] = jnp.zeros((WIN, SHIFT, channels), F32)
        attn_cols[:, SHIFT : SHIFT + ncol] = attn.reshape(WIN, ncol, channels)
        for i in range(WIN):
            attn_edge[i * SHIFT : (i + 1) * SHIFT] = attn_cols[i, ncol : ncol + SHIFT]
        wt = dot(ct, attn_cols[:, :ncol].reshape(rows, channels).astype(BF16), 0, 0)
        wt = wt + dot(edge, attn_edge[...].astype(BF16), 0, 0)
        halves = wt.reshape(d // 16, 2, 8, channels)
        first = core == 0
        low, high = halves[:, 0].astype(BF16), halves[:, 1].astype(BF16)
        keep_ref[g, : d // 16] = jnp.where(first, low, high)
        send_ref[g, : d // 16] = jnp.where(first, high, low)

        diag = [jnp.zeros((8, 128), F32) for _ in range(heads)]
        for a in range(WIN):
            for p in range(heads // 2):
                block = ds_total[8 * a : 8 * a + 8, 128 * p : 128 * p + 128]
                lo = jnp.where(lane128 < 64, block, 0.0)
                hi = jnp.where(lane128 < 64, 0.0, block)
                diag[2 * p] = diag[2 * p] + pltpu.roll(lo, (7 - a) * 8, 1)
                diag[2 * p + 1] = diag[2 * p + 1] + pltpu.roll(hi, ((7 - a) * 8 - 64) % 128, 1)
        evens = [jnp.where(even_lane, t, 0.0) for t in diag]
        odds = [jnp.where(even_lane, 0.0, t) for t in diag]
        total = jnp.zeros((8, 128), F32)
        for b in range(WIN):
            line = jnp.concatenate([t[b : b + 1] for t in evens + odds], 0)
            total = total + pltpu.roll(line, 7 - b, 1)
        both = jnp.concatenate([total, jnp.zeros((8, channels - 128), F32)], 1)
        both = both.astype(BF16)
        keep_ref[g, d // 16] = both
        send_ref[g, d // 16] = both
        for result in results[2 + 2 * g : 4 + 2 * g]:
            result.start()

    for g in range(groups):
        group(g)
    for result in results:
        result.wait()


def attention(flags, tokens, grads, strips, weights, halves, table, gain, valids):
    channels, d = weights[1].shape
    own = grads[0].shape[0]
    ncol = own // strips[0].shape[0]
    piece = jax.ShapeDtypeStruct((2, d // 16 + 1, 8, channels), BF16)
    term = jax.ShapeDtypeStruct((2 * own, d), BF16)
    vmem = pl.BlockSpec(memory_space=pltpu.VMEM)
    hbm = pl.BlockSpec(memory_space=pltpu.HBM)
    return pl.pallas_call(
        attention_kernel,
        out_shape=(term, term, piece, piece),
        in_specs=[pl.BlockSpec(memory_space=pltpu.SMEM)] + [hbm] * 10 + [vmem] * 4,
        out_specs=(hbm,) * 4,
        scratch_shapes=[
            pltpu.VMEM(piece.shape, BF16),
            pltpu.VMEM(piece.shape, BF16),
            pltpu.VMEM((2, own, d), BF16),
            pltpu.VMEM((2, own, d), BF16),
            pltpu.VMEM((2,) + strips[0].shape, BF16),
            pltpu.VMEM((2 * own, d), BF16),
            pltpu.VMEM((WIN, ncol + WIN, d), F32),
            pltpu.VMEM((WIN * SHIFT, d), F32),
            pltpu.VMEM((2, 3, d, channels), BF16),
            pltpu.VMEM((2, channels, d), BF16),
            pltpu.VMEM((2, 2 * own, d), F32),
            pltpu.VMEM((2, 2 * own, d), BF16),
            pltpu.VMEM((WIN, ncol + WIN, channels), F32),
            pltpu.VMEM((WIN, ncol + WIN, channels), F32),
            pltpu.VMEM((WIN * SHIFT, channels), F32),
            pltpu.VMEM((16, channels), BF16),
            pltpu.SemaphoreType.DMA((2 * (3 + d // channels) + 15,)),
        ],
        compiler_params=pltpu.CompilerParams(vmem_limit_bytes=MAIN_VMEM_LIMIT),
        cost_estimate=pl.CostEstimate(
            flops=3_000_000_000, bytes_accessed=11_000_000, transcendentals=131072
        ),
        name="window_attention",
    )(flags, *tokens, *grads, *strips, *weights, *halves, table, gain, *valids)


def pack_kernel(core_ref, wq_ref, wp_ref, tab_ref, out_ref):
    tall, d = wp_ref.shape
    _, half, channels = wq_ref.shape
    for t in range(3):
        out_ref[t * half : (t + 1) * half] = wq_ref[t]
    for j in range(d // channels):
        at = 3 * half + j * tall
        out_ref[at : at + tall] = wp_ref[:, j * channels : (j + 1) * channels]
    table = table_to_rows(tab_ref[...])
    top = table.astype(BF16)
    table = table - top.astype(F32)
    middle = table.astype(BF16)
    table = table - middle.astype(F32)
    low = jnp.concatenate([table, jnp.zeros_like(table)], 1)
    high = jnp.concatenate([top.astype(F32), middle.astype(F32)], 1)
    at = out_ref.shape[0] - 2 * table.shape[0]
    out_ref[at:, : high.shape[1]] = jnp.concatenate([high, low], 0).astype(BF16)


def packed_half(core, w_qkv, w_proj, table):
    _, d, channels = w_qkv.shape
    rows = 3 * d // 2 + d // channels * (channels // 2) + 4 * table.shape[0]
    return pl.pallas_call(
        pack_kernel,
        out_shape=jax.ShapeDtypeStruct((rows, channels), BF16),
        grid_spec=pltpu.PrefetchScalarGridSpec(
            num_scalar_prefetch=1,
            grid=(1,),
            in_specs=[
                pl.BlockSpec((3, d // 2, channels), lambda i, core: (0, core[0], 0)),
                pl.BlockSpec((channels // 2, d), lambda i, core: (core[0], 0)),
                pl.BlockSpec(table.shape, lambda i, core: (0, 0)),
            ],
            out_specs=pl.BlockSpec((rows, channels), lambda i, core: (0, 0)),
        ),
        compiler_params=pltpu.CompilerParams(vmem_limit_bytes=VMEM_LIMIT),
        cost_estimate=pl.CostEstimate(flops=0, bytes_accessed=2_100_000, transcendentals=0),
        name="packed_half",
    )(core, w_qkv, w_proj, table)


def strips_kernel(tokens_ref, grads_ref, out_ref):
    out_ref[...] = jnp.concatenate([tokens_ref[:, :SHIFT], grads_ref[:, :SHIFT]], 1)


def left_strips(tokens, grads):
    prow, ncol, d = tokens.shape
    spec = pl.BlockSpec((prow, 16, d), lambda i: (0, 0, 0))
    return pl.pallas_call(
        strips_kernel,
        grid=(1,),
        out_shape=jax.ShapeDtypeStruct((prow, 2 * SHIFT, d), BF16),
        in_specs=[spec, spec],
        out_specs=pl.BlockSpec((prow, 2 * SHIFT, d), lambda i: (0, 0, 0)),
        compiler_params=pltpu.CompilerParams(vmem_limit_bytes=STRIPS_VMEM_LIMIT),
        cost_estimate=pl.CostEstimate(flops=0, bytes_accessed=300_000, transcendentals=0),
        name="left_strips",
    )(tokens, grads)


def on_device(tokens, valid, gain, w_qkv, w_proj, rel_table, cotangent):
    part_rows, ncol, d = tokens.shape
    n_head = lax.axis_size("head")
    n_row = lax.axis_size("row")
    n_col = lax.axis_size("col")
    tile_rows = part_rows * n_head
    own = part_rows * ncol
    strip = part_rows * SHIFT
    channels = w_proj.shape[0]
    row = lax.axis_index("row")
    col = lax.axis_index("col")
    head = lax.axis_index("head")

    right = [(c, (c + 1) % n_col) for c in range(n_col)]
    swap = [(c, c ^ 1) for c in range(n_col)]
    mates = []
    for r in range(n_row):
        low, high = r * n_head, (r + 1) % n_row * n_head
        mates += [(low + 1, low + 2), (low + 2, low + 1), (low + 3, high), (high, low + 3)]
    beside = [(h, h ^ 1) for h in range(n_head)]

    def trade(value):
        return lax.ppermute(value, ("row", "head"), mates)

    last = ((head == 3) & (row == n_row - 1)) | ((head == 0) & (row == 0))
    inner = (head == 1) | (head == 2)
    flags = [last, col == n_col - 1, col % 2 == 1, head % 2 == 0, jnp.logical_not(inner), head == 0]
    flags = jnp.stack([flag.astype(jnp.int32) for flag in flags])
    table = rel_table.T
    w_qkv = w_qkv.transpose(1, 0, 2)

    half = lax.ppermute(packed_half((col % 2)[None], w_qkv, w_proj, table), "head", beside)
    strips = left_strips(tokens, cotangent)
    whole = ("row", "col", "head")
    holder = {a: b for a, b in mates}

    def place(line_head, c):
        return (line_head // n_head * n_col + c) * n_head + line_head % n_head

    spots = [(i, c) for i in range(n_row * n_head) for c in range(n_col)]
    straight = [(place(i, (c + 1) % n_col), place(i, c)) for i, c in spots]
    across = [(place(holder[i], (c + 1) % n_col), place(i, c)) for i, c in spots]
    strips = (lax.ppermute(strips, whole, straight), lax.ppermute(strips, whole, across))
    grads = cotangent.reshape(own, d)
    grads = (grads, trade(grads))
    patches = tokens.reshape(own, d)
    patches = (patches, trade(patches))
    marks = valid.astype(F32)
    down = [(r * n_head, (r + 1) % n_row * n_head) for r in range(n_row)]
    marks = (marks, lax.ppermute(marks, ("row", "head"), down))
    half, *_ = lax.optimization_barrier((half, patches[1], grads[1], *strips, marks[1]))
    other_half = lax.ppermute(half, "col", swap)

    own_term, mate_term, keep, send = attention(
        flags,
        patches,
        grads,
        strips,
        (w_qkv, w_proj),
        (half, other_half),
        table,
        gain[None],
        marks,
    )
    pairs = keep.astype(F32) + lax.ppermute(send, "col", swap).astype(F32)
    mate_term = trade(mate_term)
    pair_beside = lax.ppermute(pairs[1].astype(BF16), "head", beside)
    pair = pairs[0] + pair_beside.astype(F32)

    table_part = jnp.broadcast_to(pair[-1:, :, :128], (d // 16, 8, 128))
    pieces = jnp.concatenate([pair[:-1], table_part], 2).astype(BF16)
    cores = [
        [r * n_col + c for r in range(n_row) for c in range(n_col) if c % 2 == parity]
        for parity in range(2)
    ]
    mate_term, _ = lax.optimization_barrier((mate_term, pieces))
    pieces = lax.all_to_all(pieces, ("row", "col"), 0, 0, axis_index_groups=cores, tiled=True)
    pieces = jnp.sum(pieces.astype(F32), 0)
    scale = 1.0 / math.sqrt(tile_rows * ncol * n_row * n_col)
    proj_grad = pieces[:, :channels].T * scale
    table_grad = rows_to_table(pieces[:, channels:]) * (WIN * scale)

    total = own_term.astype(F32) + mate_term.astype(F32)
    total = total.reshape(2, part_rows, ncol, d)
    edges = lax.ppermute(total[:, :, -SHIFT:].astype(BF16), "col", right).astype(F32)
    total = jnp.concatenate([edges, total[:, :, :-SHIFT]], 2)
    norm_grad = total[0]

    flat = tokens.astype(F32)
    mean = jnp.mean(flat, -1, keepdims=True)
    centered = flat - mean
    rstd = lax.rsqrt(jnp.mean(centered * centered, -1, keepdims=True) + EPS)
    xhat = centered * rstd
    scaled = norm_grad * gain
    token_gradient = cotangent.astype(F32) + rstd * (
        scaled
        - jnp.mean(scaled, -1, keepdims=True)
        - xhat * jnp.mean(scaled * xhat, -1, keepdims=True)
    )

    mixed = (flat + total[1]).astype(BF16)
    return (mixed, token_gradient.astype(BF16), proj_grad, table_grad)


def solution(mesh):
    return jax.shard_map(
        on_device,
        mesh=mesh,
        in_specs=(
            P(("row", "head"), "col", None),
            P("row", "col"),
            P(),
            P(None, None, "head"),
            P("head", None),
            P(None, "head"),
            P(("row", "head"), "col", None),
        ),
        out_specs=(
            P(("row", "head"), "col", None),
            P(("row", "head"), "col", None),
            P("head", ("row", "col")),
            P(None, "head"),
        ),
        check_vma=False,
    )
```
